32 devices in a mesh: pulse: 4 (over z), tile: 8 (over y, x, core).
Axes of the slice: x: 2, y: 2, z: 4, core: 2. Of those that a mesh axis runs over, the one named last changes fastest.
Arguments:
- echoes: bfloat16 [2, 128, 4, 16384], P(None, 'pulse', None, 'tile'), may hold values from -6 to 6
- replica: bfloat16 [2, 2048], replicated, may hold values from -0.09375 to 0.09375
- steer_phase: float32 [16, 16], replicated, may hold values from -3.140625 to 3.140625
- range_shift: int32 [2, 32], replicated, may hold values from -8 to 7
- merge_phase: float32 [2, 32], replicated, may hold values from -3.140625 to 3.140625
- merge_frac: float32 [2, 32], replicated, may hold values from 0 to 1
- footprint: int32 [4, 128], P('pulse', 'tile'), may hold values from 0 to 7, as said below
- row_slot: int32 [4, 128], P('pulse', 'tile'), may hold values from 0 to 15
- beam_index: int32 [4, 128, 128], P('pulse', 'tile'), may hold values from 0 to 30
- beam_frac: bfloat16 [4, 128, 128], P('pulse', 'tile'), may hold values from 0 to 1
Outputs:
- image: bfloat16 [2, 4, 128, 16384], P(None, None, 'pulse', 'tile')
The draws below stay inside these ranges and needn't reach their ends.
Inputs may be any that keep to these rules, and one draw needn't show every extreme that they name: `footprint`: of the 16 blocks of one tile and one pulse block, at most 2 fall on any one tile; in every draw one tile receives exactly 2 blocks from every tile and pulse block.
All inputs are finite; a program needn't handle non-finite values.
Results may differ from the reference program's by a relative error of at most 0.018.
Values may be sent and summed in bfloat16 or wider, within the bound.
A program may use at most 128 MiB of HBM per device.

```python
import math
import jax
import jax.numpy as jnp
from jax import lax

POL = 4
TAPS = 2048
SUBLEN = 16
BEAMS = 16
REACH = 8
RBLOCK = 128
FBEAMS = 128
CAP = 2
PULSES = 128
RANGE = 16384
SUBS = 2
MSUBS = 1
CHILD = 32
NBLK = 16
PBLOCKS = 4
FOOT = 128


def draw_footprint(key, part):
    tiles = FOOT // NBLK
    hottest = jax.random.randint(jax.random.fold_in(key, 7), (), 0, tiles)

    def one_device(device):
        dev_key = jax.random.fold_in(key, device + 11)
        first_key, second_key = jax.random.split(dev_key)
        others = jnp.arange((tiles - 1) * CAP, dtype=jnp.int32) // CAP
        others = others + (others >= hottest).astype(jnp.int32)
        others = jax.random.permutation(first_key, others)
        chosen = jnp.concatenate([jnp.zeros((CAP,), jnp.int32) + hottest, others[:NBLK - CAP]])
        return jax.random.permutation(second_key, chosen)
    listing = jax.vmap(one_device)(jnp.arange(PBLOCKS * tiles, dtype=jnp.int32))
    return listing.reshape(PBLOCKS, FOOT).astype(jnp.int32)


def touch_ends(result, rng, low, high):
    longest = result.shape.index(max(result.shape))
    spots = []
    for shift in (0, 1):
        where = [jax.random.randint(jax.random.fold_in(rng, axis), (), 0, length) for axis, length in enumerate(result.shape)]
        where[longest] = (where[longest] + shift) % result.shape[longest]
        spots.append(tuple(where))
    return result.at[spots[0]].set(low).at[spots[1]].set(high)


def level_of(own_key, dims, cuts, smallest, top_value):
    def one(axis_at, parts):
        draws = jax.random.uniform(jax.random.fold_in(jax.random.fold_in(own_key, 6), axis_at), (parts,), jnp.float32, smallest / len(cuts), top_value / len(cuts))
        return jnp.repeat(jnp.exp(draws), dims[axis_at] // parts).reshape((-1,) + (1,) * (len(dims) - axis_at - 1))

    loudness = one(*cuts[0])
    for cut in cuts[1:]:
        loudness = loudness * one(*cut)
    return loudness


def centred(own_key, shape, width, bound, cuts=(), kind=jnp.bfloat16):
    entries = width * jax.random.normal(own_key, shape, jnp.float32)
    if cuts:
        entries = entries * level_of(own_key, shape, cuts, -0.22, 0.18)
    return jnp.clip(entries, -bound, bound).astype(kind)


def setup_inputs(seed: int = 0) -> dict:
    key_list = jax.random.split(jax.random.key(seed), 11)
    echoes = centred(key_list[0], (2, PULSES, POL, RANGE), 1.0, 6.0, ((1, 4), (3, 8)))
    replica = centred(key_list[1], (2, TAPS), (2 * TAPS) ** -0.5, 0.09375)
    steer_phase = jnp.clip(jax.random.uniform(key_list[2], (BEAMS, SUBLEN), jnp.float32, -3.140625, 3.140625), -3.140625, 3.140625)
    range_shift = touch_ends(jax.random.randint(key_list[3], (2, 2 * BEAMS), 0 - REACH, REACH), jax.random.fold_in(key_list[3], 1), 0 - REACH, REACH - 1).astype(jnp.int32)
    merge_phase = jnp.clip(jax.random.uniform(key_list[4], (2, 2 * BEAMS), jnp.float32, -3.140625, 3.140625), -3.140625, 3.140625)
    merge_frac = jnp.clip(jax.random.uniform(key_list[5], (2, 2 * BEAMS), jnp.float32, 0.0, 1.0), 0.0, 1.0)
    footprint = draw_footprint(jax.random.fold_in(key_list[10], 71), 0)
    row_slot = touch_ends(jax.random.randint(key_list[7], (PBLOCKS, FOOT), 0, NBLK), jax.random.fold_in(key_list[7], 1), 0, NBLK - 1).astype(jnp.int32)
    beam_index = touch_ends(jax.random.randint(key_list[8], (PBLOCKS, FOOT, FBEAMS), 0, CHILD - 1), jax.random.fold_in(key_list[8], 1), 0, (CHILD - 1) - 1).astype(jnp.int32)
    beam_frac = jnp.clip(1.0 * jax.random.uniform(key_list[9], (PBLOCKS, FOOT, FBEAMS), jnp.float32) ** level_of(key_list[9], (PBLOCKS, FOOT, FBEAMS), ((0, 4), (1, 8)), -0.2, 0.2), 0.0, 1.0).astype(jnp.bfloat16)
    return dict(echoes=echoes, replica=replica, steer_phase=steer_phase, range_shift=range_shift, merge_phase=merge_phase, merge_frac=merge_frac, footprint=footprint, row_slot=row_slot, beam_index=beam_index, beam_frac=beam_frac)


def merge_pairs(padded, range_shift, merge_phase, merge_frac, extent):
    half_root = math.sqrt(0.5)
    total = None
    for parity in range(2):
        source = padded[:, parity::2]

        def single(beam_at, shift_at, angle, weight):
            picked = lax.dynamic_index_in_dim(source, beam_at // 2, axis=3, keepdims=False)
            lower_bins = lax.dynamic_slice_in_dim(picked, shift_at + REACH, extent, axis=3).astype(jnp.float32)
            upper_bins = lax.dynamic_slice_in_dim(picked, shift_at + REACH + 1, extent, axis=3).astype(jnp.float32)
            blended = (1.0 - weight) * lower_bins + weight * upper_bins
            cosine = jnp.cos(angle) * half_root
            sine = jnp.sin(angle) * half_root
            return jnp.stack([cosine * blended[0] - sine * blended[1], cosine * blended[1] + sine * blended[0]])
        beam_ids = jnp.arange(range_shift.shape[1], dtype=jnp.int32)
        branch = jax.vmap(single, out_axes=3)(beam_ids, range_shift[parity], merge_phase[parity], merge_frac[parity])
        total = branch if total is None else total + branch
    return total

def reference(echoes, replica, steer_phase, range_shift, merge_phase, merge_frac, footprint, row_slot, beam_index, beam_frac):
    tap_count = replica.shape[1]
    total_range = echoes.shape[3]
    fft_length = total_range + tap_count
    signal = echoes[0].astype(jnp.float32) + 1j * echoes[1].astype(jnp.float32)
    kernel = replica[0].astype(jnp.float32) + 1j * replica[1].astype(jnp.float32)
    spectrum = jnp.fft.fft(signal, n=fft_length, axis=-1) * jnp.conj(jnp.fft.fft(kernel, n=fft_length))
    correlated = jnp.fft.ifft(spectrum, axis=-1)[..., :total_range]
    compressed = jnp.stack([correlated.real, correlated.imag]).astype(jnp.bfloat16)
    scale = 1.0 / math.sqrt(SUBLEN)
    steer_re = (jnp.cos(steer_phase) * scale).astype(jnp.bfloat16).astype(jnp.float32)
    steer_im = (jnp.sin(steer_phase) * scale).astype(jnp.bfloat16).astype(jnp.float32)
    grouped_all = compressed.reshape(2, PBLOCKS, SUBS, SUBLEN, POL, total_range).transpose(1, 0, 2, 3, 4, 5)

    def per_block(accum, items):
        grouped, foot, rows_at, index_tab, frac_tab = items
        grouped = grouped.astype(jnp.float32)
        sub_re = jnp.einsum('ap,spqr->sqar', steer_re, grouped[0]) - jnp.einsum('ap,spqr->sqar', steer_im, grouped[1])
        sub_im = jnp.einsum('ap,spqr->sqar', steer_re, grouped[1]) + jnp.einsum('ap,spqr->sqar', steer_im, grouped[0])
        subimage = jnp.stack([sub_re, sub_im]).astype(jnp.bfloat16)
        padded = jnp.pad(subimage, ((0, 0), (0, 0), (0, 0), (0, 0), (REACH, REACH)))
        merged = merge_pairs(padded, range_shift, merge_phase, merge_frac, total_range).astype(jnp.bfloat16)
        children = merged.reshape(2, MSUBS, POL, 2 * BEAMS, FOOT, RBLOCK).transpose(4, 0, 2, 1, 3, 5)
        children = children.reshape(FOOT, 2, POL, CHILD, RBLOCK)
        lower = (1.0 - frac_tab.astype(jnp.float32)).astype(jnp.bfloat16)
        full_shape = (FOOT, 2, POL, FBEAMS, RBLOCK)
        low_index = jnp.broadcast_to(index_tab[:, None, None, :, None], full_shape)
        low_vals = jnp.take_along_axis(children, low_index, axis=3).astype(jnp.float32)
        high_vals = jnp.take_along_axis(children, low_index + 1, axis=3).astype(jnp.float32)
        resampled = lower.astype(jnp.float32)[:, None, None, :, None] * low_vals + frac_tab.astype(jnp.float32)[:, None, None, :, None] * high_vals
        segment = (foot * NBLK + rows_at).astype(jnp.int32)
        placed = jax.ops.segment_sum(resampled, segment, num_segments=FOOT)
        partial_value = placed.transpose(1, 2, 3, 0, 4).reshape(2, POL, FBEAMS, total_range).astype(jnp.bfloat16)
        return (accum + partial_value.astype(jnp.float32), None)
    start_image = jnp.zeros((2, POL, FBEAMS, total_range), jnp.float32)
    summed, _ = lax.scan(per_block, start_image, (grouped_all, footprint, row_slot, beam_index, beam_frac))
    return summed.astype(jnp.bfloat16)
```

```python
import functools
import math

import jax
import jax.numpy as jnp
from jax import lax
from jax.experimental import pallas as pl
from jax.experimental.pallas import tpu as pltpu
from jax.sharding import PartitionSpec as P

RBLOCK = 128
CAP = 2
CBLOCK = 256
EDGE = 128
TABROWS = 16


def shifted(value, axis, by):
    count = lax.axis_size(axis)
    pairs = [(i, i + by) for i in range(count) if 0 <= i + by < count]
    return lax.ppermute(value, axis, pairs)


def iota(shape, dim):
    return lax.broadcasted_iota(jnp.int32, shape, dim)


def form_kernel(
    shift_ref, coef_ref, foot_ref, slot_ref,
    own_ref, next_ref, prev_ref, after_ref, replica_ref, steer_ref, index_ref, frac_ref,
    out_ref,
    ext_ref, toep_ref, sub_ref, merged_ref,
):
    range_dev = own_ref.shape[2]
    rows = own_ref.shape[1]
    taps = replica_ref.shape[1]
    window = CBLOCK + taps
    width = sub_ref.shape[1]
    blocks = range_dev // RBLOCK
    bf16 = jnp.bfloat16

    ext_ref[:, :, 0:EDGE] = prev_ref[...]
    ext_ref[:, :, EDGE : EDGE + range_dev] = own_ref[...]
    ext_ref[:, :, EDGE + range_dev : EDGE + 2 * range_dev] = next_ref[...]
    ext_ref[:, :, EDGE + 2 * range_dev :] = after_ref[...]

    for part in range(2):
        line = replica_ref[part : part + 1, :].astype(jnp.float32)
        line = jnp.concatenate([line, jnp.zeros((1, CBLOCK), jnp.float32)], axis=1)
        rolled = pltpu.roll(
            jnp.broadcast_to(line, (CBLOCK, window)), 0, 1, stride=1, stride_axis=0
        )
        if part == 0:
            toep_ref[0:CBLOCK, 0:window] = rolled.astype(bf16)
            toep_ref[CBLOCK:, window:] = rolled.astype(bf16)
        else:
            toep_ref[0:CBLOCK, window:] = rolled.astype(bf16)
            toep_ref[CBLOCK:, 0:window] = (-rolled).astype(bf16)

    r_at = iota((256, 32), 0)
    left = (((r_at >> 2) & 1) * 16 + ((r_at >> 3) & 15) == iota((256, 32), 1)).astype(bf16)
    k_at = iota((32, 256), 1)
    right = ((k_at >> 7) * 16 + ((k_at >> 2) & 15) == iota((32, 256), 0)).astype(bf16)
    spread = jnp.dot(left, steer_ref[...], preferred_element_type=jnp.float32).astype(bf16)
    spread = jnp.dot(spread, right, preferred_element_type=jnp.float32)
    r_all, k_all = iota((256, 256), 0), iota((256, 256), 1)
    same = ((r_all >> 7) == ((k_all >> 6) & 1)) & ((r_all & 3) == (k_all & 3))
    steer = jnp.where(same, spread, 0.0).astype(bf16)

    group = 3

    def compress(at, carry):
        pieces = []
        for step in range(group):
            start = pl.multiple_of((at * group + step) * CBLOCK, CBLOCK)
            pieces.append(
                jnp.concatenate(
                    [ext_ref[0, :, pl.ds(start, window)], ext_ref[1, :, pl.ds(start, window)]],
                    axis=1,
                )
            )
        left_side = jnp.concatenate(pieces, axis=0)
        found = lax.dot_general(
            left_side, toep_ref[...], (((1,), (1,)), ((), ())),
            preferred_element_type=jnp.float32,
        ).astype(bf16)
        for step in range(group):
            start = pl.multiple_of((at * group + step) * CBLOCK, CBLOCK)
            one = found[step * rows : (step + 1) * rows]
            stacked = jnp.concatenate([one[:, :CBLOCK], one[:, CBLOCK:]], axis=0)
            sub = jnp.dot(steer, stacked, preferred_element_type=jnp.float32)
            sub_ref[:, pl.ds(start, CBLOCK)] = sub.astype(bf16).astype(jnp.float32)
        return carry

    lax.fori_loop(0, width // (CBLOCK * group), compress, 0)

    @pl.when(lax.axis_index("tile") == 0)
    def _():
        sub_ref[:, 0:EDGE] = jnp.zeros((256, EDGE), jnp.float32)

    sign = jnp.where(iota((8, width), 0) < 4, -1.0, 1.0).astype(jnp.float32)

    def merge(a, carry):
        totals = [None, None]
        for c in range(2):
            x = sub_ref[pl.ds(pl.multiple_of((c * 16 + a) * 8, 8), 8), :]
            x_up = pltpu.roll(x, width - 1, 1)
            for parity in range(2):
                b = 2 * a + parity
                weight = coef_ref[0, c * 32 + b]
                cosine = coef_ref[1, c * 32 + b]
                sine = coef_ref[2, c * 32 + b]
                y = (1.0 - weight) * x + weight * x_up
                v = cosine * y + (sine * sign) * pltpu.roll(y, 4, 0)
                by = shift_ref[c, b]
                z = pltpu.roll(v, jnp.where(by > 0, width - by, -by), 1)
                z = z[:, EDGE : EDGE + range_dev]
                totals[parity] = z if totals[parity] is None else totals[parity] + z
        merged_ref[pl.ds(pl.multiple_of(a * 16, 16), 16), :] = jnp.concatenate(
            totals, axis=0
        ).astype(bf16)
        return carry

    lax.fori_loop(0, 16, merge, 0)

    order = (k_all == (r_all & 31) * 8 + (r_all >> 5)).astype(bf16)
    if out_ref.shape[0] > blocks:
        out_ref[...] = jnp.zeros(out_ref.shape, bf16)
    tab_row = iota((TABROWS, RBLOCK), 0)
    for f in range(blocks):
        foot = foot_ref[0, f]
        rank = jnp.int32(0)
        for before in range(f):
            rank = rank + (foot_ref[0, before] == foot).astype(jnp.int32)
        slot = foot * CAP + rank
        part = jnp.dot(
            order, merged_ref[:, f * RBLOCK : (f + 1) * RBLOCK],
            preferred_element_type=jnp.float32,
        )
        out_ref[slot, 0:256, :] = part.astype(bf16)
        landing = (slot_ref[0, f] + 1).astype(jnp.float32)
        index_f = index_ref[0, f : f + 1, :].astype(jnp.float32)
        frac_f = frac_ref[0, f : f + 1, :].astype(jnp.float32)
        table = jnp.where(tab_row == 0, index_f, jnp.where(tab_row == 1, frac_f, 0.0))
        table = jnp.where(tab_row == 2, landing, table)
        out_ref[slot, 256 : 256 + TABROWS, :] = table.astype(bf16)


def place_kernel(got_ref, out_ref, left_ref, right_ref):
    slots = got_ref.shape[0]
    beams = out_ref.shape[1]
    spans = out_ref.shape[2] // RBLOCK
    lanes = spans * beams
    mine = lax.axis_index("pulse") * beams
    bf16 = jnp.bfloat16
    lane = iota((RBLOCK, lanes), 1)
    widen = ((lane & (beams - 1)) + mine == iota((RBLOCK, lanes), 0)).astype(bf16)
    where_at = iota((1, lanes), 1) // beams + 1
    child = iota((32, lanes), 0).astype(jnp.float32)

    def prepare(at, carry):
        table = got_ref[at, 256 : 256 + TABROWS, :]
        wide = jnp.dot(table, widen, preferred_element_type=jnp.float32)
        landing = wide[2:3, :]
        index = jnp.where(landing == where_at.astype(jnp.float32), wide[0:1, :], -9.0)
        frac = wide[1:2, :]
        lower = (1.0 - frac).astype(bf16).astype(jnp.float32)
        weight = jnp.where(child == index, lower, 0.0)
        weight = jnp.where(child == index + 1.0, frac, weight)
        start = pl.multiple_of(at * 32, 32)
        left_ref[pl.ds(start, 32), :] = weight.astype(bf16)
        for x in range(8):
            right_ref[pl.ds(start, 32), x * RBLOCK : (x + 1) * RBLOCK] = got_ref[
                at, x * 32 : (x + 1) * 32, :
            ]
        return carry

    lax.fori_loop(0, slots, prepare, 0)
    for half in range(0, lanes, 256):
        result = lax.dot_general(
            left_ref[:, half : half + 256], right_ref[...], (((0,), (0,)), ((), ())),
            preferred_element_type=jnp.float32,
        ).astype(bf16)
        for sub in range(256 // beams):
            w = half // beams + sub
            for x in range(8):
                out_ref[x, :, w * RBLOCK : (w + 1) * RBLOCK] = result[
                    sub * beams : (sub + 1) * beams, x * RBLOCK : (x + 1) * RBLOCK
                ]


def shards(
    echoes, replica, steer_phase, range_shift, merge_phase, merge_frac,
    footprint, row_slot, beam_index, beam_frac,
):
    pulse_count, pol_count, range_dev = echoes.shape[1:]
    rows = pulse_count * pol_count
    taps = replica.shape[1]
    final_beams = beam_index.shape[2]
    tiles = lax.axis_size("tile")
    groups = lax.axis_size("pulse")
    slot_count = tiles * CAP
    own = echoes.reshape(2, rows, range_dev)
    following = shifted(own, "tile", -1)
    before = shifted(own[:, :, range_dev - EDGE :], "tile", 1)
    after = shifted(own[:, :, :EDGE], "tile", -2)

    scale = 1.0 / math.sqrt(steer_phase.shape[1])
    steer_re = jnp.cos(steer_phase) * scale
    steer_im = jnp.sin(steer_phase) * scale
    steer = jnp.concatenate(
        [
            jnp.concatenate([steer_re, -steer_im], axis=1),
            jnp.concatenate([steer_im, steer_re], axis=1),
        ],
        axis=0,
    ).astype(jnp.bfloat16)
    half_root = math.sqrt(0.5)
    coef = jnp.stack(
        [
            merge_frac.reshape(-1),
            (jnp.cos(merge_phase) * half_root).reshape(-1),
            (jnp.sin(merge_phase) * half_root).reshape(-1),
        ]
    )
    width = range_dev + CBLOCK
    smem = pl.BlockSpec(memory_space=pltpu.SMEM)
    vmem = pl.BlockSpec(memory_space=pltpu.VMEM)
    sent = pl.pallas_call(
        form_kernel,
        out_shape=jax.ShapeDtypeStruct((slot_count, 256 + TABROWS, RBLOCK), jnp.bfloat16),
        in_specs=[smem] * 4 + [vmem] * 8,
        out_specs=vmem,
        scratch_shapes=[
            pltpu.VMEM((2, rows, 2 * range_dev + 2 * EDGE), jnp.bfloat16),
            pltpu.VMEM((2 * CBLOCK, 2 * (CBLOCK + taps)), jnp.bfloat16),
            pltpu.VMEM((256, width), jnp.float32),
            pltpu.VMEM((256, range_dev), jnp.bfloat16),
        ],
        compiler_params=pltpu.CompilerParams(vmem_limit_bytes=56 << 20),
    )(
        range_shift, coef, footprint, row_slot,
        own, following, before, after, replica, steer, beam_index, beam_frac,
    )
    got = lax.all_to_all(
        sent.reshape(tiles, CAP, 256 + TABROWS, RBLOCK), "tile",
        split_axis=0, concat_axis=0, tiled=True,
    ).reshape(slot_count, 256 + TABROWS, RBLOCK)
    gathered = lax.all_gather(got, "pulse", axis=0, tiled=True)
    beams = final_beams // groups
    total_slots = groups * slot_count
    image = pl.pallas_call(
        place_kernel,
        out_shape=jax.ShapeDtypeStruct((2 * pol_count, beams, range_dev), jnp.bfloat16),
        in_specs=[vmem],
        out_specs=vmem,
        scratch_shapes=[
            pltpu.VMEM((total_slots * 32, range_dev // RBLOCK * beams), jnp.bfloat16),
            pltpu.VMEM((total_slots * 32, 8 * RBLOCK), jnp.bfloat16),
        ],
        compiler_params=pltpu.CompilerParams(vmem_limit_bytes=56 << 20),
    )(gathered)
    return image.reshape(2, pol_count, beams, range_dev)


def solution(mesh):
    placed = (
        P(None, "pulse", None, "tile"),
        P(),
        P(),
        P(),
        P(),
        P(),
        P("pulse", "tile"),
        P("pulse", "tile"),
        P("pulse", "tile", None),
        P("pulse", "tile", None),
    )
    return jax.shard_map(
        shards,
        mesh=mesh,
        in_specs=placed,
        out_specs=P(None, None, "pulse", "tile"),
        check_vma=False,
    )
```

```python
import functools
import math

import jax
import jax.numpy as jnp
from jax import lax
from jax.experimental import pallas as pl
from jax.experimental.pallas import tpu as pltpu
from jax.sharding import PartitionSpec as P

RBLOCK = 128
CAP = 2
CBLOCK = 256
EDGE = 128
TABROWS = 16


def shifted(value, axis, by):
    count = lax.axis_size(axis)
    pairs = [(i, i + by) for i in range(count) if 0 <= i + by < count]
    return lax.ppermute(value, axis, pairs)


def iota(shape, dim):
    return lax.broadcasted_iota(jnp.int32, shape, dim)


def form_kernel(
    shift_ref, coef_ref, foot_ref, slot_ref,
    own_ref, next_ref, prev_ref, after_ref, replica_ref, steer_ref, index_ref, frac_ref,
    kid_ref, tab_ref,
    ext_ref, toep_ref, sub_ref, merged_ref,
):
    range_dev = own_ref.shape[2]
    rows = own_ref.shape[1]
    taps = replica_ref.shape[1]
    window = CBLOCK + taps
    width = sub_ref.shape[1]
    blocks = range_dev // RBLOCK
    bf16 = jnp.bfloat16

    ext_ref[:, :, 0:EDGE] = prev_ref[...]
    ext_ref[:, :, EDGE : EDGE + range_dev] = own_ref[...]
    ext_ref[:, :, EDGE + range_dev : EDGE + 2 * range_dev] = next_ref[...]
    ext_ref[:, :, EDGE + 2 * range_dev :] = after_ref[...]

    for part in range(2):
        line = replica_ref[part : part + 1, :].astype(jnp.float32)
        line = jnp.concatenate([line, jnp.zeros((1, CBLOCK), jnp.float32)], axis=1)
        rolled = pltpu.roll(
            jnp.broadcast_to(line, (CBLOCK, window)), 0, 1, stride=1, stride_axis=0
        )
        if part == 0:
            toep_ref[0:CBLOCK, 0:window] = rolled.astype(bf16)
            toep_ref[CBLOCK:, window:] = rolled.astype(bf16)
        else:
            toep_ref[0:CBLOCK, window:] = rolled.astype(bf16)
            toep_ref[CBLOCK:, 0:window] = (-rolled).astype(bf16)

    r_at = iota((256, 32), 0)
    left = (((r_at >> 2) & 1) * 16 + ((r_at >> 3) & 15) == iota((256, 32), 1)).astype(bf16)
    k_at = iota((32, 256), 1)
    right = ((k_at >> 7) * 16 + ((k_at >> 2) & 15) == iota((32, 256), 0)).astype(bf16)
    spread = jnp.dot(left, steer_ref[...], preferred_element_type=jnp.float32).astype(bf16)
    spread = jnp.dot(spread, right, preferred_element_type=jnp.float32)
    r_all, k_all = iota((256, 256), 0), iota((256, 256), 1)
    same = ((r_all >> 7) == ((k_all >> 6) & 1)) & ((r_all & 3) == (k_all & 3))
    steer = jnp.where(same, spread, 0.0).astype(bf16)

    group = 3

    def compress(at, carry):
        pieces = []
        for step in range(group):
            start = pl.multiple_of((at * group + step) * CBLOCK, CBLOCK)
            pieces.append(
                jnp.concatenate(
                    [ext_ref[0, :, pl.ds(start, window)], ext_ref[1, :, pl.ds(start, window)]],
                    axis=1,
                )
            )
        left_side = jnp.concatenate(pieces, axis=0)
        found = lax.dot_general(
            left_side, toep_ref[...], (((1,), (1,)), ((), ())),
            preferred_element_type=jnp.float32,
        ).astype(bf16)
        for step in range(group):
            start = pl.multiple_of((at * group + step) * CBLOCK, CBLOCK)
            one = found[step * rows : (step + 1) * rows]
            stacked = jnp.concatenate([one[:, :CBLOCK], one[:, CBLOCK:]], axis=0)
            sub = jnp.dot(steer, stacked, preferred_element_type=jnp.float32)
            sub_ref[:, pl.ds(start, CBLOCK)] = sub.astype(bf16).astype(jnp.float32)
        return carry

    lax.fori_loop(0, width // (CBLOCK * group), compress, 0)

    @pl.when(lax.axis_index("tile") == 0)
    def _():
        sub_ref[:, 0:EDGE] = jnp.zeros((256, EDGE), jnp.float32)

    sign = jnp.where(iota((8, width), 0) < 4, -1.0, 1.0).astype(jnp.float32)

    def merge(a, carry):
        totals = [None, None]
        for c in range(2):
            x = sub_ref[pl.ds(pl.multiple_of((c * 16 + a) * 8, 8), 8), :]
            x_up = pltpu.roll(x, width - 1, 1)
            for parity in range(2):
                b = 2 * a + parity
                weight = coef_ref[0, c * 32 + b]
                cosine = coef_ref[1, c * 32 + b]
                sine = coef_ref[2, c * 32 + b]
                y = (1.0 - weight) * x + weight * x_up
                v = cosine * y + (sine * sign) * pltpu.roll(y, 4, 0)
                by = shift_ref[c, b]
                z = pltpu.roll(v, jnp.where(by > 0, width - by, -by), 1)
                z = z[:, EDGE : EDGE + range_dev]
                totals[parity] = z if totals[parity] is None else totals[parity] + z
        merged_ref[pl.ds(pl.multiple_of(a * 16, 16), 16), :] = jnp.concatenate(
            totals, axis=0
        ).astype(bf16)
        return carry

    lax.fori_loop(0, 16, merge, 0)

    order = (k_all == (r_all & 31) * 8 + (r_all >> 5)).astype(bf16)
    if tab_ref.shape[0] > blocks:
        kid_ref[...] = jnp.zeros(kid_ref.shape, bf16)
        tab_ref[...] = jnp.zeros(tab_ref.shape, bf16)
    tab_row = iota((TABROWS, RBLOCK), 0)
    for f in range(blocks):
        foot = foot_ref[0, f]
        rank = jnp.int32(0)
        for before in range(f):
            rank = rank + (foot_ref[0, before] == foot).astype(jnp.int32)
        slot = foot * CAP + rank
        part = jnp.dot(
            order, merged_ref[:, f * RBLOCK : (f + 1) * RBLOCK],
            preferred_element_type=jnp.float32,
        )
        kid_ref[:, slot] = part.astype(bf16).reshape(8, 32, RBLOCK)
        landing = (slot_ref[0, f] + 1).astype(jnp.float32)
        index_f = index_ref[0, f : f + 1, :].astype(jnp.float32)
        frac_f = frac_ref[0, f : f + 1, :].astype(jnp.float32)
        table = jnp.where(tab_row == 0, index_f, jnp.where(tab_row == 1, frac_f, 0.0))
        table = jnp.where(tab_row == 2, landing, table)
        tab_ref[slot] = table.astype(bf16)


def place_kernel(got_ref, out_ref, left_ref, right_ref):
    slots = got_ref.shape[0]
    beams = out_ref.shape[1]
    spans = out_ref.shape[2] // RBLOCK
    lanes = spans * beams
    mine = lax.axis_index("pulse") * beams
    bf16 = jnp.bfloat16
    lane = iota((RBLOCK, lanes), 1)
    widen = ((lane & (beams - 1)) + mine == iota((RBLOCK, lanes), 0)).astype(bf16)
    where_at = iota((1, lanes), 1) // beams + 1
    child = iota((32, lanes), 0).astype(jnp.float32)

    def prepare(at, carry):
        table = got_ref[at, 256 : 256 + TABROWS, :]
        wide = jnp.dot(table, widen, preferred_element_type=jnp.float32)
        landing = wide[2:3, :]
        index = jnp.where(landing == where_at.astype(jnp.float32), wide[0:1, :], -9.0)
        frac = wide[1:2, :]
        lower = (1.0 - frac).astype(bf16).astype(jnp.float32)
        weight = jnp.where(child == index, lower, 0.0)
        weight = jnp.where(child == index + 1.0, frac, weight)
        start = pl.multiple_of(at * 32, 32)
        left_ref[pl.ds(start, 32), :] = weight.astype(bf16)
        for x in range(8):
            right_ref[pl.ds(start, 32), x * RBLOCK : (x + 1) * RBLOCK] = got_ref[
                at, x * 32 : (x + 1) * 32, :
            ]
        return carry

    lax.fori_loop(0, slots, prepare, 0)
    for half in range(0, lanes, 256):
        result = lax.dot_general(
            left_ref[:, half : half + 256], right_ref[...], (((0,), (0,)), ((), ())),
            preferred_element_type=jnp.float32,
        ).astype(bf16)
        for sub in range(256 // beams):
            w = half // beams + sub
            for x in range(8):
                out_ref[x, :, w * RBLOCK : (w + 1) * RBLOCK] = result[
                    sub * beams : (sub + 1) * beams, x * RBLOCK : (x + 1) * RBLOCK
                ]


CHUNKS = 4
MESH = pl.DeviceIdType.MESH


def line_kernel(
    tiles, kid_ref, tab_ref, out_ref,
    kids, tabs, left_ref, part_ref, arrived_ref, own_ref,
    a2a_send, a2a_recv, line_send, line_recv, part_send, part_recv, local_sem,
):
    g = lax.axis_index("pulse")
    t = lax.axis_index("tile")
    beams = out_ref.shape[1]
    spans = out_ref.shape[2] // RBLOCK
    lanes = spans * beams
    slots = tiles * CAP
    depth = slots * 32
    per = 8 // CHUNKS
    bf16 = jnp.bfloat16
    f32 = jnp.float32
    is_mid = (g == 1) | (g == 2)
    inner = jnp.where(g == 0, 1, jnp.where(g == 1, 2, jnp.where(g == 2, 1, 2)))
    end = jnp.where(g < 2, 0, 3)
    far = 3 - end

    barrier = pltpu.get_barrier_semaphore()
    for d in range(1, tiles):
        pl.semaphore_signal(
            barrier, inc=1, device_id={"tile": lax.rem(t + d, tiles)}, device_id_type=MESH
        )
    pl.semaphore_signal(barrier, inc=1, device_id={"pulse": inner}, device_id_type=MESH)

    @pl.when(is_mid)
    def _():
        pl.semaphore_signal(barrier, inc=1, device_id={"pulse": end}, device_id_type=MESH)
        pl.semaphore_wait(barrier, tiles + 1)

    @pl.when(jnp.logical_not(is_mid))
    def _():
        pl.semaphore_wait(barrier, tiles)

    def spread_copy(k, d, peer, place):
        if k == CHUNKS:
            src = tab_ref.at[pl.ds(peer * CAP, CAP)]
            dst = tabs.at[g, pl.ds(place * CAP, CAP)]
        else:
            src = kid_ref.at[pl.ds(k * per, per), pl.ds(peer * CAP, CAP)]
            dst = kids.at[g, pl.ds(k * per, per), pl.ds(place * CAP, CAP)]
        return pltpu.make_async_remote_copy(
            src_ref=src, dst_ref=dst,
            send_sem=a2a_send.at[k, d - 1], recv_sem=a2a_recv.at[k, d - 1],
            device_id={"tile": peer}, device_id_type=MESH,
        )

    order = [CHUNKS] + list(range(CHUNKS))
    for k in order:
        for d in range(1, tiles):
            spread_copy(k, d, lax.rem(t + d, tiles), t).start()
    keep_tab = pltpu.make_async_copy(
        tab_ref.at[pl.ds(t * CAP, CAP)], tabs.at[g, pl.ds(t * CAP, CAP)], local_sem.at[0]
    )
    keep_kid = pltpu.make_async_copy(
        kid_ref.at[:, pl.ds(t * CAP, CAP)], kids.at[g, :, pl.ds(t * CAP, CAP)], local_sem.at[1]
    )
    keep_tab.start()
    keep_kid.start()
    keep_tab.wait()
    keep_kid.wait()

    def spread_wait(k):
        for d in range(1, tiles):
            peer = lax.rem(t + tiles - d, tiles)
            spread_copy(k, d, peer, peer).wait_recv()

    def line_copy(k, group, lane, to):
        if k == CHUNKS:
            part = tabs.at[group]
        else:
            part = kids.at[group, pl.ds(k * per, per)]
        return pltpu.make_async_remote_copy(
            src_ref=part, dst_ref=part,
            send_sem=line_send.at[lane, k], recv_sem=line_recv.at[group, k],
            device_id={"pulse": to}, device_id_type=MESH,
        )

    def part_copy(k, to):
        return pltpu.make_async_remote_copy(
            src_ref=part_ref.at[pl.ds(k * per, per)],
            dst_ref=arrived_ref.at[pl.ds(k * per, per)],
            send_sem=part_send.at[k], recv_sem=part_recv.at[k],
            device_id={"pulse": to}, device_id_type=MESH,
        )

    def prepare(group, beam_group, row, column, used):
        expand = (
            (iota((RBLOCK, lanes), 1) & (beams - 1)) + beam_group * beams
            == iota((RBLOCK, lanes), 0)
        ).astype(bf16)
        where_at = (iota((1, lanes), 1) // beams + 1).astype(f32)
        child = iota((32, lanes), 0).astype(f32)

        def four(at, carry):
            pieces = []
            for step in range(4):
                wide = jnp.dot(
                    tabs[group, at * 4 + step], expand, preferred_element_type=f32
                )
                index = jnp.where((wide[2:3, :] == where_at) & used, wide[0:1, :], -9.0)
                frac = wide[1:2, :]
                lower = (1.0 - frac).astype(bf16).astype(f32)
                weight = jnp.where(child == index, lower, 0.0)
                pieces.append(jnp.where(child == index + 1.0, frac, weight))
            block = jnp.concatenate(pieces, axis=0)
            at_column = pl.multiple_of(column + at * 128, 128)
            left_ref[row : row + lanes, pl.ds(at_column, 128)] = block.T.astype(bf16)
            return carry

        lax.fori_loop(0, slots // 4, four, 0)

    @pl.when(is_mid)
    def _():
        def begin(k):
            spread_wait(k)
            line_copy(k, g, 0, inner).start()
            line_copy(k, end, 0, inner).wait_recv()
            line_copy(k, end, 1, inner).start()

        def finish(k):
            line_copy(k, inner, 0, inner).wait_recv()
            line_copy(k, far, 0, inner).wait_recv()

        begin(CHUNKS)
        begin(0)
        finish(CHUNKS)

        def prepare_group(group, carry):
            column = pl.multiple_of(group * depth, 128)
            prepare(group, g, 0, column, group >= 0)
            prepare(group, end, lanes, column, group != end)
            return carry

        lax.fori_loop(0, 4, prepare_group, 0)
        for k in range(CHUNKS):
            if k + 1 < CHUNKS:
                begin(k + 1)
            finish(k)
            right = jnp.concatenate(
                [kids[:, k * per + i].reshape(4 * depth, RBLOCK) for i in range(per)], axis=1
            )
            result = jnp.dot(
                left_ref[lanes:, :], right, preferred_element_type=f32
            ).astype(bf16)
            for w in range(spans):
                for i in range(per):
                    part_ref[k * per + i, :, w * RBLOCK : (w + 1) * RBLOCK] = result[
                        w * beams : (w + 1) * beams, i * RBLOCK : (i + 1) * RBLOCK
                    ]
            part_copy(k, end).start()
            result = jnp.dot(
                left_ref[:lanes, :], right, preferred_element_type=f32
            ).astype(bf16)
            for w in range(spans):
                for i in range(per):
                    out_ref[k * per + i, :, w * RBLOCK : (w + 1) * RBLOCK] = result[
                        w * beams : (w + 1) * beams, i * RBLOCK : (i + 1) * RBLOCK
                    ]
        for k in order:
            line_copy(k, g, 0, inner).wait_send()
            line_copy(k, end, 1, inner).wait_send()
        for k in range(CHUNKS):
            part_copy(k, end).wait_send()

    @pl.when(jnp.logical_not(is_mid))
    def _():
        for k in order:
            spread_wait(k)
            line_copy(k, g, 0, inner).start()
        prepare(g, g, 0, 0, g >= 0)
        for k in range(CHUNKS):
            right = jnp.concatenate(
                [kids[g, k * per + i].reshape(depth, RBLOCK) for i in range(per)], axis=1
            )
            result = jnp.dot(
                left_ref[:lanes, :depth], right, preferred_element_type=f32
            )
            for w in range(spans):
                for i in range(per):
                    own_ref[k * per + i, :, w * RBLOCK : (w + 1) * RBLOCK] = result[
                        w * beams : (w + 1) * beams, i * RBLOCK : (i + 1) * RBLOCK
                    ]
        for k in range(CHUNKS):
            part_copy(k, inner).wait_recv()
            for i in range(per):
                x = k * per + i
                out_ref[x] = (own_ref[x] + arrived_ref[x].astype(f32)).astype(bf16)
        for k in order:
            line_copy(k, g, 0, inner).wait_send()

    for k in order:
        for d in range(1, tiles):
            spread_copy(k, d, lax.rem(t + d, tiles), t).wait_send()


def line_exchange(kids, tabs, tiles, beams, range_dev):
    slots = tiles * CAP
    lanes = range_dev // RBLOCK * beams
    bf16 = jnp.bfloat16
    vmem = pl.BlockSpec(memory_space=pltpu.VMEM)
    dma = pltpu.SemaphoreType.DMA
    return pl.pallas_call(
        functools.partial(line_kernel, tiles),
        out_shape=jax.ShapeDtypeStruct((8, beams, range_dev), bf16),
        in_specs=[vmem, vmem],
        out_specs=vmem,
        scratch_shapes=[
            pltpu.VMEM((4, 8, slots, 32, RBLOCK), bf16),
            pltpu.VMEM((4, slots, TABROWS, RBLOCK), bf16),
            pltpu.VMEM((2 * lanes, 4 * slots * 32), bf16),
            pltpu.VMEM((8, beams, range_dev), bf16),
            pltpu.VMEM((8, beams, range_dev), bf16),
            pltpu.VMEM((8, beams, range_dev), jnp.float32),
            dma((CHUNKS + 1, tiles - 1)),
            dma((CHUNKS + 1, tiles - 1)),
            dma((2, CHUNKS + 1)),
            dma((4, CHUNKS + 1)),
            dma((CHUNKS,)),
            dma((CHUNKS,)),
            dma((2,)),
        ],
        compiler_params=pltpu.CompilerParams(
            collective_id=0, has_side_effects=True, vmem_limit_bytes=56 << 20
        ),
    )(kids, tabs)


def shards(
    echoes, replica, steer_phase, range_shift, merge_phase, merge_frac,
    footprint, row_slot, beam_index, beam_frac,
):
    pulse_count, pol_count, range_dev = echoes.shape[1:]
    rows = pulse_count * pol_count
    taps = replica.shape[1]
    final_beams = beam_index.shape[2]
    tiles = lax.axis_size("tile")
    groups = lax.axis_size("pulse")
    slot_count = tiles * CAP
    own = echoes.reshape(2, rows, range_dev)
    following = shifted(own, "tile", -1)
    before = shifted(own[:, :, range_dev - EDGE :], "tile", 1)
    after = shifted(own[:, :, :EDGE], "tile", -2)

    scale = 1.0 / math.sqrt(steer_phase.shape[1])
    steer_re = jnp.cos(steer_phase) * scale
    steer_im = jnp.sin(steer_phase) * scale
    steer = jnp.concatenate(
        [
            jnp.concatenate([steer_re, -steer_im], axis=1),
            jnp.concatenate([steer_im, steer_re], axis=1),
        ],
        axis=0,
    ).astype(jnp.bfloat16)
    half_root = math.sqrt(0.5)
    coef = jnp.stack(
        [
            merge_frac.reshape(-1),
            (jnp.cos(merge_phase) * half_root).reshape(-1),
            (jnp.sin(merge_phase) * half_root).reshape(-1),
        ]
    )
    width = range_dev + CBLOCK
    smem = pl.BlockSpec(memory_space=pltpu.SMEM)
    vmem = pl.BlockSpec(memory_space=pltpu.VMEM)
    kids, tabs = pl.pallas_call(
        form_kernel,
        out_shape=(
            jax.ShapeDtypeStruct((8, slot_count, 32, RBLOCK), jnp.bfloat16),
            jax.ShapeDtypeStruct((slot_count, TABROWS, RBLOCK), jnp.bfloat16),
        ),
        in_specs=[smem] * 4 + [vmem] * 8,
        out_specs=(vmem, vmem),
        scratch_shapes=[
            pltpu.VMEM((2, rows, 2 * range_dev + 2 * EDGE), jnp.bfloat16),
            pltpu.VMEM((2 * CBLOCK, 2 * (CBLOCK + taps)), jnp.bfloat16),
            pltpu.VMEM((256, width), jnp.float32),
            pltpu.VMEM((256, range_dev), jnp.bfloat16),
        ],
        compiler_params=pltpu.CompilerParams(vmem_limit_bytes=56 << 20),
    )(
        range_shift, coef, footprint, row_slot,
        own, following, before, after, replica, steer, beam_index, beam_frac,
    )
    beams = final_beams // groups
    if groups == 4:
        image = line_exchange(kids, tabs, tiles, beams, range_dev)
        return image.reshape(2, pol_count, beams, range_dev)
    sent = jnp.concatenate(
        [kids.transpose(1, 0, 2, 3).reshape(slot_count, 256, RBLOCK), tabs], axis=1
    )
    got = lax.all_to_all(
        sent.reshape(tiles, CAP, 256 + TABROWS, RBLOCK), "tile",
        split_axis=0, concat_axis=0, tiled=True,
    ).reshape(slot_count, 256 + TABROWS, RBLOCK)
    gathered = lax.all_gather(got, "pulse", axis=0, tiled=True)
    total_slots = groups * slot_count
    image = pl.pallas_call(
        place_kernel,
        out_shape=jax.ShapeDtypeStruct((2 * pol_count, beams, range_dev), jnp.bfloat16),
        in_specs=[vmem],
        out_specs=vmem,
        scratch_shapes=[
            pltpu.VMEM((total_slots * 32, range_dev // RBLOCK * beams), jnp.bfloat16),
            pltpu.VMEM((total_slots * 32, 8 * RBLOCK), jnp.bfloat16),
        ],
        compiler_params=pltpu.CompilerParams(vmem_limit_bytes=56 << 20),
    )(gathered)
    return image.reshape(2, pol_count, beams, range_dev)


def solution(mesh):
    placed = (
        P(None, "pulse", None, "tile"),
        P(),
        P(),
        P(),
        P(),
        P(),
        P("pulse", "tile"),
        P("pulse", "tile"),
        P("pulse", "tile", None),
        P("pulse", "tile", None),
    )
    return jax.shard_map(
        shards,
        mesh=mesh,
        in_specs=placed,
        out_specs=P(None, None, "pulse", "tile"),
        check_vma=False,
    )
```

```python
import functools
import math

import jax
import jax.numpy as jnp
from jax import lax
from jax.experimental import pallas as pl
from jax.experimental.pallas import tpu as pltpu
from jax.sharding import PartitionSpec as P

RBLOCK = 128
CAP = 2
CBLOCK = 256
EDGE = 128
TABROWS = 16


def shifted(value, axis, by):
    count = lax.axis_size(axis)
    pairs = [(i, i + by) for i in range(count) if 0 <= i + by < count]
    return lax.ppermute(value, axis, pairs)


def iota(shape, dim):
    return lax.broadcasted_iota(jnp.int32, shape, dim)


def form_kernel(
    shift_ref, coef_ref, foot_ref, slot_ref,
    own_ref, next_ref, prev_ref, after_ref, replica_ref, steer_ref, index_ref, frac_ref,
    kid_ref, tab_ref,
    ext_ref, toep_ref, sub_ref, merged_ref,
):
    range_dev = own_ref.shape[2]
    rows = own_ref.shape[1]
    taps = replica_ref.shape[1]
    window = CBLOCK + taps
    width = sub_ref.shape[1]
    blocks = range_dev // RBLOCK
    bf16 = jnp.bfloat16

    ext_ref[:, :, 0:EDGE] = prev_ref[...]
    ext_ref[:, :, EDGE : EDGE + range_dev] = own_ref[...]
    ext_ref[:, :, EDGE + range_dev : EDGE + 2 * range_dev] = next_ref[...]
    ext_ref[:, :, EDGE + 2 * range_dev :] = after_ref[...]

    for part in range(2):
        line = replica_ref[part : part + 1, :].astype(jnp.float32)
        line = jnp.concatenate([line, jnp.zeros((1, CBLOCK), jnp.float32)], axis=1)
        rolled = pltpu.roll(
            jnp.broadcast_to(line, (CBLOCK, window)), 0, 1, stride=1, stride_axis=0
        )
        if part == 0:
            toep_ref[0:CBLOCK, 0:window] = rolled.astype(bf16)
            toep_ref[CBLOCK:, window:] = rolled.astype(bf16)
        else:
            toep_ref[0:CBLOCK, window:] = rolled.astype(bf16)
            toep_ref[CBLOCK:, 0:window] = (-rolled).astype(bf16)

    r_at = iota((256, 32), 0)
    left = (((r_at >> 2) & 1) * 16 + ((r_at >> 3) & 15) == iota((256, 32), 1)).astype(bf16)
    k_at = iota((32, 256), 1)
    right = ((k_at >> 7) * 16 + ((k_at >> 2) & 15) == iota((32, 256), 0)).astype(bf16)
    spread = jnp.dot(left, steer_ref[...], preferred_element_type=jnp.float32).astype(bf16)
    spread = jnp.dot(spread, right, preferred_element_type=jnp.float32)
    r_all, k_all = iota((256, 256), 0), iota((256, 256), 1)
    same = ((r_all >> 7) == ((k_all >> 6) & 1)) & ((r_all & 3) == (k_all & 3))
    steer = jnp.where(same, spread, 0.0).astype(bf16)

    group = 3

    def compress(at, carry):
        pieces = []
        for step in range(group):
            start = pl.multiple_of((at * group + step) * CBLOCK, CBLOCK)
            pieces.append(
                jnp.concatenate(
                    [ext_ref[0, :, pl.ds(start, window)], ext_ref[1, :, pl.ds(start, window)]],
                    axis=1,
                )
            )
        left_side = jnp.concatenate(pieces, axis=0)
        found = lax.dot_general(
            left_side, toep_ref[...], (((1,), (1,)), ((), ())),
            preferred_element_type=jnp.float32,
        ).astype(bf16)
        for step in range(group):
            start = pl.multiple_of((at * group + step) * CBLOCK, CBLOCK)
            one = found[step * rows : (step + 1) * rows]
            stacked = jnp.concatenate([one[:, :CBLOCK], one[:, CBLOCK:]], axis=0)
            sub = jnp.dot(steer, stacked, preferred_element_type=jnp.float32)
            sub_ref[:, pl.ds(start, CBLOCK)] = sub.astype(bf16).astype(jnp.float32)
        return carry

    lax.fori_loop(0, width // (CBLOCK * group), compress, 0)

    @pl.when(lax.axis_index("tile") == 0)
    def _():
        sub_ref[:, 0:EDGE] = jnp.zeros((256, EDGE), jnp.float32)

    sign = jnp.where(iota((8, width), 0) < 4, -1.0, 1.0).astype(jnp.float32)

    def merge(a, carry):
        totals = [None, None]
        for c in range(2):
            x = sub_ref[pl.ds(pl.multiple_of((c * 16 + a) * 8, 8), 8), :]
            x_up = pltpu.roll(x, width - 1, 1)
            for parity in range(2):
                b = 2 * a + parity
                weight = coef_ref[0, c * 32 + b]
                cosine = coef_ref[1, c * 32 + b]
                sine = coef_ref[2, c * 32 + b]
                y = (1.0 - weight) * x + weight * x_up
                v = cosine * y + (sine * sign) * pltpu.roll(y, 4, 0)
                by = shift_ref[c, b]
                z = pltpu.roll(v, jnp.where(by > 0, width - by, -by), 1)
                z = z[:, EDGE : EDGE + range_dev]
                totals[parity] = z if totals[parity] is None else totals[parity] + z
        merged_ref[pl.ds(pl.multiple_of(a * 16, 16), 16), :] = jnp.concatenate(
            totals, axis=0
        ).astype(bf16)
        return carry

    lax.fori_loop(0, 16, merge, 0)

    order = (k_all == (r_all & 31) * 8 + (r_all >> 5)).astype(bf16)
    if tab_ref.shape[0] > blocks:
        kid_ref[...] = jnp.zeros(kid_ref.shape, bf16)
        tab_ref[...] = jnp.zeros(tab_ref.shape, bf16)
    tab_row = iota((TABROWS, RBLOCK), 0)
    for f in range(blocks):
        foot = foot_ref[0, f]
        rank = jnp.int32(0)
        for before in range(f):
            rank = rank + (foot_ref[0, before] == foot).astype(jnp.int32)
        slot = foot * CAP + rank
        part = jnp.dot(
            order, merged_ref[:, f * RBLOCK : (f + 1) * RBLOCK],
            preferred_element_type=jnp.float32,
        )
        kid_ref[:, slot] = part.astype(bf16).reshape(8, 32, RBLOCK)
        landing = (slot_ref[0, f] + 1).astype(jnp.float32)
        index_f = index_ref[0, f : f + 1, :].astype(jnp.float32)
        frac_f = frac_ref[0, f : f + 1, :].astype(jnp.float32)
        table = jnp.where(tab_row == 0, index_f, jnp.where(tab_row == 1, frac_f, 0.0))
        table = jnp.where(tab_row == 2, landing, table)
        tab_ref[slot] = table.astype(bf16)


def place_kernel(got_ref, out_ref, left_ref, right_ref):
    slots = got_ref.shape[0]
    beams = out_ref.shape[1]
    spans = out_ref.shape[2] // RBLOCK
    lanes = spans * beams
    mine = lax.axis_index("pulse") * beams
    bf16 = jnp.bfloat16
    lane = iota((RBLOCK, lanes), 1)
    widen = ((lane & (beams - 1)) + mine == iota((RBLOCK, lanes), 0)).astype(bf16)
    where_at = iota((1, lanes), 1) // beams + 1
    child = iota((32, lanes), 0).astype(jnp.float32)

    def prepare(at, carry):
        table = got_ref[at, 256 : 256 + TABROWS, :]
        wide = jnp.dot(table, widen, preferred_element_type=jnp.float32)
        landing = wide[2:3, :]
        index = jnp.where(landing == where_at.astype(jnp.float32), wide[0:1, :], -9.0)
        frac = wide[1:2, :]
        lower = (1.0 - frac).astype(bf16).astype(jnp.float32)
        weight = jnp.where(child == index, lower, 0.0)
        weight = jnp.where(child == index + 1.0, frac, weight)
        start = pl.multiple_of(at * 32, 32)
        left_ref[pl.ds(start, 32), :] = weight.astype(bf16)
        for x in range(8):
            right_ref[pl.ds(start, 32), x * RBLOCK : (x + 1) * RBLOCK] = got_ref[
                at, x * 32 : (x + 1) * 32, :
            ]
        return carry

    lax.fori_loop(0, slots, prepare, 0)
    for half in range(0, lanes, 256):
        result = lax.dot_general(
            left_ref[:, half : half + 256], right_ref[...], (((0,), (0,)), ((), ())),
            preferred_element_type=jnp.float32,
        ).astype(bf16)
        for sub in range(256 // beams):
            w = half // beams + sub
            for x in range(8):
                out_ref[x, :, w * RBLOCK : (w + 1) * RBLOCK] = result[
                    sub * beams : (sub + 1) * beams, x * RBLOCK : (x + 1) * RBLOCK
                ]


CHUNKS = 4
MESH = pl.DeviceIdType.MESH


STAGES = 2


def fused_kernel(
    tiles, shift_ref, coef_ref, foot_ref,
    echo_ref, replica_ref, steer_ref, table_ref, out_ref,
    ext_ref, toep_ref, sub_ref, merged_ref, block_ref, kid_ref, tab_ref,
    kids, tabs, left_ref, part_ref, arrived_ref, own_ref,
    halo_send, halo_recv,
    a2a_send, a2a_recv, line_send, line_recv, part_send, part_recv,
):
    g = lax.axis_index("pulse")
    t = lax.axis_index("tile")
    beams = out_ref.shape[1]
    spans = out_ref.shape[2] // RBLOCK
    lanes = spans * beams
    slots = tiles * CAP
    depth = slots * 32
    per = 8 // CHUNKS
    bf16 = jnp.bfloat16
    f32 = jnp.float32
    is_mid = (g == 1) | (g == 2)
    inner = jnp.where(g == 0, 1, jnp.where(g == 1, 2, jnp.where(g == 2, 1, 2)))
    end = jnp.where(g < 2, 0, 3)
    far = 3 - end

    barrier = pltpu.get_barrier_semaphore()
    for d in range(1, tiles):
        pl.semaphore_signal(
            barrier, inc=1, device_id={"tile": lax.rem(t + d, tiles)}, device_id_type=MESH
        )
    pl.semaphore_signal(barrier, inc=1, device_id={"pulse": inner}, device_id_type=MESH)

    @pl.when(is_mid)
    def _():
        pl.semaphore_signal(barrier, inc=1, device_id={"pulse": end}, device_id_type=MESH)
        pl.semaphore_wait(barrier, tiles + 1)

    @pl.when(jnp.logical_not(is_mid))
    def _():
        pl.semaphore_wait(barrier, tiles)

    range_dev = echo_ref.shape[3]
    rows = echo_ref.shape[2]
    taps = replica_ref.shape[1]
    window = CBLOCK + taps
    width = sub_ref.shape[1]
    blocks = range_dev // RBLOCK

    halos = [
        ((0, range_dev), EDGE + range_dev, -1),
        ((range_dev - EDGE, EDGE), 0, 1),
        ((0, EDGE), EDGE + 2 * range_dev, -2),
    ]

    def halo_copy(stage, j):
        (first, count), to, by = halos[j]
        return pltpu.make_async_remote_copy(
            src_ref=echo_ref.at[stage, :, :, pl.ds(first, count)],
            dst_ref=ext_ref.at[stage, :, :, pl.ds(to, count)],
            send_sem=halo_send.at[stage, j], recv_sem=halo_recv.at[stage, j],
            device_id={"tile": lax.rem(t + by + tiles, tiles)}, device_id_type=MESH,
        )

    def sends(j):
        by = halos[j][2]
        return (t + by >= 0) & (t + by < tiles)

    def gets(j):
        by = halos[j][2]
        return (t - by >= 0) & (t - by < tiles)

    for stage in range(STAGES):
        for j in range(3):
            @pl.when(sends(j))
            def _():
                halo_copy(stage, j).start()

    for stage in range(STAGES):
        for j in range(3):
            (_, count), to, _ = halos[j]

            @pl.when(jnp.logical_not(gets(j)))
            def _():
                ext_ref[stage, :, :, to : to + count] = jnp.zeros((2, rows, count), bf16)

        ext_ref[stage, :, :, EDGE : EDGE + range_dev] = echo_ref[stage]

    for part in range(2):
        line = replica_ref[part : part + 1, :].astype(f32)
        line = jnp.concatenate([line, jnp.zeros((1, CBLOCK), f32)], axis=1)
        rolled = pltpu.roll(
            jnp.broadcast_to(line, (CBLOCK, window)), 0, 1, stride=1, stride_axis=0
        )
        if part == 0:
            toep_ref[0:CBLOCK, 0:window] = rolled.astype(bf16)
            toep_ref[CBLOCK:, window:] = rolled.astype(bf16)
        else:
            toep_ref[0:CBLOCK, window:] = rolled.astype(bf16)
            toep_ref[CBLOCK:, 0:window] = (-rolled).astype(bf16)

    r_at = iota((256, 32), 0)
    turn, want = (r_at >> 2) & 1, (r_at >> 1) & 1
    picked = jnp.where(turn == 1, 1 - want, want)
    left = ((picked * 16 + ((r_at >> 3) & 15)) == iota((256, 32), 1)).astype(f32)
    left = jnp.where((turn == 1) & (want == 0), -left, left).astype(bf16)
    k_at = iota((32, 128), 1)
    right = ((k_at >> 6) * 16 + ((k_at >> 1) & 15) == iota((32, 128), 0)).astype(bf16)
    spread = jnp.dot(left, steer_ref[...], preferred_element_type=f32).astype(bf16)
    spread = jnp.dot(spread, right, preferred_element_type=f32)
    r_all, k_all = iota((256, 128), 0), iota((256, 128), 1)
    same = ((r_all >> 7) == ((k_all >> 5) & 1)) & ((r_all & 1) == (k_all & 1))
    steer = jnp.where(same, spread, 0.0).astype(bf16)
    o_all, i_all = iota((128, 128), 0), iota((128, 128), 1)
    order_in = (o_all & 31) * 4 + ((o_all >> 5) & 1) * 2 + (o_all >> 6)
    reorder = (i_all == order_in).astype(bf16)

    targets = []
    for f in range(blocks):
        rank = jnp.int32(0)
        for earlier in range(f):
            rank = rank + (foot_ref[0, earlier] == foot_ref[0, f]).astype(jnp.int32)
        targets.append(foot_ref[0, f] * CAP + rank)
    sources = []
    for s in range(slots):
        source = jnp.int32(0)
        for f in range(blocks):
            source = source + f * (targets[f] == s).astype(jnp.int32)
        sources.append(source)
    for s in range(slots):
        tab_ref[s] = table_ref[sources[s]]

    group = 3

    def form(stage, between):
        for j in range(3):
            @pl.when(gets(j))
            def _():
                halo_copy(stage, j).wait_recv()

        def compress(at, carry):
            pieces = []
            for step in range(group):
                start = pl.multiple_of((at * group + step) * CBLOCK, CBLOCK)
                pieces.append(
                    jnp.concatenate(
                        [
                            ext_ref[stage, 0, :, pl.ds(start, window)],
                            ext_ref[stage, 1, :, pl.ds(start, window)],
                        ],
                        axis=1,
                    )
                )
            found = lax.dot_general(
                jnp.concatenate(pieces, axis=0), toep_ref[...], (((1,), (1,)), ((), ())),
                preferred_element_type=f32,
            ).astype(bf16)
            for step in range(group):
                start = pl.multiple_of((at * group + step) * CBLOCK, CBLOCK)
                one = found[step * rows : (step + 1) * rows]
                stacked = jnp.concatenate([one[:, :CBLOCK], one[:, CBLOCK:]], axis=0)
                sub = jnp.dot(steer, stacked, preferred_element_type=f32)
                sub_ref[:, pl.ds(start, CBLOCK)] = sub.astype(bf16).astype(f32)
            return carry

        lax.fori_loop(0, width // (CBLOCK * group), compress, 0)

        @pl.when(t == 0)
        def _():
            sub_ref[:, 0:EDGE] = jnp.zeros((256, EDGE), f32)

        between()

        def merge(a, carry):
            totals = [None, None]
            for c in range(2):
                x = sub_ref[pl.ds(pl.multiple_of((c * 16 + a) * 8, 8), 8), :]
                x_up = pltpu.roll(x, width - 1, 1)
                for parity in range(2):
                    b = 2 * a + parity
                    weight = coef_ref[0, c * 32 + b]
                    cosine = coef_ref[1, c * 32 + b]
                    sine = coef_ref[2, c * 32 + b]
                    y = (1.0 - weight) * x + weight * x_up
                    v = cosine * y + sine * pltpu.roll(y, 4, 0)
                    by = shift_ref[c, b]
                    z = pltpu.roll(v, jnp.where(by > 0, width - by, -by), 1)
                    z = z[:, EDGE : EDGE + range_dev]
                    totals[parity] = z if totals[parity] is None else totals[parity] + z
            both = jnp.where(
                iota((8, range_dev), 0) < 4, totals[0], pltpu.roll(totals[1], 4, 0)
            )
            merged_ref[pl.ds(pl.multiple_of(a * 8, 8), 8), :] = both
            return carry

        lax.fori_loop(0, 16, merge, 0)
        for f in range(blocks):
            part = jnp.dot(
                reorder, merged_ref[:, f * RBLOCK : (f + 1) * RBLOCK].astype(bf16),
                preferred_element_type=f32,
            )
            block_ref[f] = part.astype(bf16).reshape(4, 32, RBLOCK)
        for s in range(slots):
            kid_ref[stage * 4 : stage * 4 + 4, s] = block_ref[sources[s]]

    def spread_copy(k, d, peer, place):
        if k == CHUNKS:
            src = tab_ref.at[pl.ds(peer * CAP, CAP)]
            dst = tabs.at[g, pl.ds(place * CAP, CAP)]
        else:
            src = kid_ref.at[pl.ds(k * per, per), pl.ds(peer * CAP, CAP)]
            dst = kids.at[g, pl.ds(k * per, per), pl.ds(place * CAP, CAP)]
        return pltpu.make_async_remote_copy(
            src_ref=src, dst_ref=dst,
            send_sem=a2a_send.at[k, d - 1], recv_sem=a2a_recv.at[k, d - 1],
            device_id={"tile": peer}, device_id_type=MESH,
        )

    order = [CHUNKS] + list(range(CHUNKS))

    def spread_start(k):
        for d in range(1, tiles):
            spread_copy(k, d, lax.rem(t + d, tiles), t).start()

    def spread_wait(k):
        for d in range(1, tiles):
            peer = lax.rem(t + tiles - d, tiles)
            spread_copy(k, d, peer, peer).wait_recv()

    def line_copy(k, group, lane, to):
        if k == CHUNKS:
            part = tabs.at[group]
        else:
            part = kids.at[group, pl.ds(k * per, per)]
        return pltpu.make_async_remote_copy(
            src_ref=part, dst_ref=part,
            send_sem=line_send.at[lane, k], recv_sem=line_recv.at[group, k],
            device_id={"pulse": to}, device_id_type=MESH,
        )

    def part_copy(k, to):
        return pltpu.make_async_remote_copy(
            src_ref=part_ref.at[pl.ds(k * per, per)],
            dst_ref=arrived_ref.at[pl.ds(k * per, per)],
            send_sem=part_send.at[k], recv_sem=part_recv.at[k],
            device_id={"pulse": to}, device_id_type=MESH,
        )

    def prepare(group, beam_group, row, column, used):
        expand = (
            (iota((RBLOCK, lanes), 1) & (beams - 1)) + beam_group * beams
            == iota((RBLOCK, lanes), 0)
        ).astype(bf16)
        where_at = (iota((1, lanes), 1) // beams + 1).astype(f32)
        child = iota((32, lanes), 0).astype(f32)

        def four(at, carry):
            pieces = []
            for step in range(4):
                wide = jnp.dot(
                    tabs[group, at * 4 + step], expand, preferred_element_type=f32
                )
                index = jnp.where((wide[2:3, :] == where_at) & used, wide[0:1, :], -9.0)
                frac = wide[1:2, :]
                lower = (1.0 - frac).astype(bf16).astype(f32)
                weight = jnp.where(child == index, lower, 0.0)
                pieces.append(jnp.where(child == index + 1.0, frac, weight))
            block = jnp.concatenate(pieces, axis=0)
            at_column = pl.multiple_of(column + at * 128, 128)
            left_ref[row : row + lanes, pl.ds(at_column, 128)] = block.T.astype(bf16)
            return carry

        lax.fori_loop(0, slots // 4, four, 0)

    def keep(k):
        if k == CHUNKS:
            tabs[g, pl.ds(t * CAP, CAP)] = tab_ref[pl.ds(t * CAP, CAP)]
        else:
            span = slice(k * per, (k + 1) * per)
            kids[g, span, pl.ds(t * CAP, CAP)] = kid_ref[span, pl.ds(t * CAP, CAP)]

    def begin_own(k):
        spread_wait(k)
        line_copy(k, g, 0, inner).start()

    spread_start(CHUNKS)
    keep(CHUNKS)
    form(0, lambda: begin_own(CHUNKS))
    for k in (0, 1):
        spread_start(k)
        keep(k)

    def between():
        begin_own(0)
        begin_own(1)

    form(1, between)
    for k in (2, 3):
        spread_start(k)
        keep(k)

    @pl.when(is_mid)
    def _():
        def relay(k):
            line_copy(k, end, 0, inner).wait_recv()
            line_copy(k, end, 1, inner).start()

        def finish(k):
            line_copy(k, inner, 0, inner).wait_recv()
            line_copy(k, far, 0, inner).wait_recv()

        relay(CHUNKS)
        relay(0)
        finish(CHUNKS)

        def prepare_group(group, carry):
            column = pl.multiple_of(group * depth, 128)
            prepare(group, g, 0, column, group >= 0)
            prepare(group, end, lanes, column, group != end)
            return carry

        lax.fori_loop(0, 4, prepare_group, 0)
        relay(1)
        begin_own(2)
        begin_own(3)
        for k in range(CHUNKS):
            if 2 <= k + 1 < CHUNKS:
                relay(k + 1)
            finish(k)
            right = jnp.concatenate(
                [kids[:, k * per + i].reshape(4 * depth, RBLOCK) for i in range(per)], axis=1
            )
            result = jnp.dot(
                left_ref[lanes:, :], right, preferred_element_type=f32
            ).astype(bf16)
            for w in range(spans):
                for i in range(per):
                    part_ref[k * per + i, :, w * RBLOCK : (w + 1) * RBLOCK] = result[
                        w * beams : (w + 1) * beams, i * RBLOCK : (i + 1) * RBLOCK
                    ]
            part_copy(k, end).start()
            result = jnp.dot(
                left_ref[:lanes, :], right, preferred_element_type=f32
            ).astype(bf16)
            for w in range(spans):
                for i in range(per):
                    out_ref[i * 4 + k, :, w * RBLOCK : (w + 1) * RBLOCK] = result[
                        w * beams : (w + 1) * beams, i * RBLOCK : (i + 1) * RBLOCK
                    ]
        for k in order:
            line_copy(k, g, 0, inner).wait_send()
            line_copy(k, end, 1, inner).wait_send()
        for k in range(CHUNKS):
            part_copy(k, end).wait_send()

    @pl.when(jnp.logical_not(is_mid))
    def _():
        begin_own(2)
        begin_own(3)
        prepare(g, g, 0, 0, g >= 0)
        for k in range(CHUNKS):
            right = jnp.concatenate(
                [kids[g, k * per + i].reshape(depth, RBLOCK) for i in range(per)], axis=1
            )
            result = jnp.dot(
                left_ref[:lanes, :depth], right, preferred_element_type=f32
            )
            for w in range(spans):
                for i in range(per):
                    own_ref[k * per + i, :, w * RBLOCK : (w + 1) * RBLOCK] = result[
                        w * beams : (w + 1) * beams, i * RBLOCK : (i + 1) * RBLOCK
                    ]
        for k in range(CHUNKS):
            part_copy(k, inner).wait_recv()
            for i in range(per):
                x = k * per + i
                out_ref[i * 4 + k] = (own_ref[x] + arrived_ref[x].astype(f32)).astype(bf16)
        for k in order:
            line_copy(k, g, 0, inner).wait_send()

    for k in order:
        for d in range(1, tiles):
            spread_copy(k, d, lax.rem(t + d, tiles), t).wait_send()
    for stage in range(STAGES):
        for j in range(3):
            @pl.when(sends(j))
            def _():
                halo_copy(stage, j).wait_send()


def fused(shift, coef, foot, echoes, replica, steer, tables, tiles, beams, range_dev):
    slots = tiles * CAP
    lanes = range_dev // RBLOCK * beams
    bf16 = jnp.bfloat16
    vmem = pl.BlockSpec(memory_space=pltpu.VMEM)
    smem = pl.BlockSpec(memory_space=pltpu.SMEM)
    dma = pltpu.SemaphoreType.DMA
    return pl.pallas_call(
        functools.partial(fused_kernel, tiles),
        out_shape=jax.ShapeDtypeStruct((8, beams, range_dev), bf16),
        in_specs=[smem] * 3 + [vmem] * 4,
        out_specs=vmem,
        scratch_shapes=[
            pltpu.VMEM(echoes.shape[:3] + (2 * range_dev + 2 * EDGE,), bf16),
            pltpu.VMEM((2 * CBLOCK, 2 * (CBLOCK + replica.shape[1])), bf16),
            pltpu.VMEM((256, range_dev + CBLOCK), jnp.float32),
            pltpu.VMEM((128, range_dev), jnp.float32),
            pltpu.VMEM((slots, 4, 32, RBLOCK), bf16),
            pltpu.VMEM((8, slots, 32, RBLOCK), bf16),
            pltpu.VMEM((slots, TABROWS, RBLOCK), bf16),
            pltpu.VMEM((4, 8, slots, 32, RBLOCK), bf16),
            pltpu.VMEM((4, slots, TABROWS, RBLOCK), bf16),
            pltpu.VMEM((2 * lanes, 4 * slots * 32), bf16),
            pltpu.VMEM((8, beams, range_dev), bf16),
            pltpu.VMEM((8, beams, range_dev), bf16),
            pltpu.VMEM((8, beams, range_dev), jnp.float32),
            dma((STAGES, 3)),
            dma((STAGES, 3)),
            dma((CHUNKS + 1, tiles - 1)),
            dma((CHUNKS + 1, tiles - 1)),
            dma((2, CHUNKS + 1)),
            dma((4, CHUNKS + 1)),
            dma((CHUNKS,)),
            dma((CHUNKS,)),
        ],
        compiler_params=pltpu.CompilerParams(
            collective_id=0, has_side_effects=True, vmem_limit_bytes=56 << 20
        ),
    )(shift, coef, foot, echoes, replica, steer, tables)


def shards(
    echoes, replica, steer_phase, range_shift, merge_phase, merge_frac,
    footprint, row_slot, beam_index, beam_frac,
):
    pulse_count, pol_count, range_dev = echoes.shape[1:]
    rows = pulse_count * pol_count
    taps = replica.shape[1]
    final_beams = beam_index.shape[2]
    tiles = lax.axis_size("tile")
    groups = lax.axis_size("pulse")
    slot_count = tiles * CAP
    scale = 1.0 / math.sqrt(steer_phase.shape[1])
    steer_re = jnp.cos(steer_phase) * scale
    steer_im = jnp.sin(steer_phase) * scale
    steer = jnp.concatenate(
        [
            jnp.concatenate([steer_re, -steer_im], axis=1),
            jnp.concatenate([steer_im, steer_re], axis=1),
        ],
        axis=0,
    ).astype(jnp.bfloat16)
    half_root = math.sqrt(0.5)
    coef = jnp.stack(
        [
            merge_frac.reshape(-1),
            (jnp.cos(merge_phase) * half_root).reshape(-1),
            (jnp.sin(merge_phase) * half_root).reshape(-1),
        ]
    )
    beams = final_beams // groups
    if groups == 4 and slot_count == range_dev // RBLOCK:
        split = echoes.reshape(2, pulse_count, STAGES, pol_count // STAGES, range_dev)
        split = split.transpose(2, 0, 1, 3, 4).reshape(STAGES, 2, rows // STAGES, range_dev)
        landing = jnp.broadcast_to(row_slot[0][:, None] + 1, beam_index.shape[1:])
        tables = jnp.stack(
            [beam_index[0].astype(jnp.float32), beam_frac[0].astype(jnp.float32),
             landing.astype(jnp.float32)], axis=1,
        )
        tables = jnp.pad(tables, ((0, 0), (0, TABROWS - 3), (0, 0))).astype(jnp.bfloat16)
        image = fused(
            range_shift, coef, footprint, split, replica, steer, tables,
            tiles, beams, range_dev,
        )
        return image.reshape(2, pol_count, beams, range_dev)
    own = echoes.reshape(2, rows, range_dev)
    following = shifted(own, "tile", -1)
    before = shifted(own[:, :, range_dev - EDGE :], "tile", 1)
    after = shifted(own[:, :, :EDGE], "tile", -2)

    width = range_dev + CBLOCK
    smem = pl.BlockSpec(memory_space=pltpu.SMEM)
    vmem = pl.BlockSpec(memory_space=pltpu.VMEM)
    kids, tabs = pl.pallas_call(
        form_kernel,
        out_shape=(
            jax.ShapeDtypeStruct((8, slot_count, 32, RBLOCK), jnp.bfloat16),
            jax.ShapeDtypeStruct((slot_count, TABROWS, RBLOCK), jnp.bfloat16),
        ),
        in_specs=[smem] * 4 + [vmem] * 8,
        out_specs=(vmem, vmem),
        scratch_shapes=[
            pltpu.VMEM((2, rows, 2 * range_dev + 2 * EDGE), jnp.bfloat16),
            pltpu.VMEM((2 * CBLOCK, 2 * (CBLOCK + taps)), jnp.bfloat16),
            pltpu.VMEM((256, width), jnp.float32),
            pltpu.VMEM((256, range_dev), jnp.bfloat16),
        ],
        compiler_params=pltpu.CompilerParams(vmem_limit_bytes=56 << 20),
    )(
        range_shift, coef, footprint, row_slot,
        own, following, before, after, replica, steer, beam_index, beam_frac,
    )
    sent = jnp.concatenate(
        [kids.transpose(1, 0, 2, 3).reshape(slot_count, 256, RBLOCK), tabs], axis=1
    )
    got = lax.all_to_all(
        sent.reshape(tiles, CAP, 256 + TABROWS, RBLOCK), "tile",
        split_axis=0, concat_axis=0, tiled=True,
    ).reshape(slot_count, 256 + TABROWS, RBLOCK)
    gathered = lax.all_gather(got, "pulse", axis=0, tiled=True)
    total_slots = groups * slot_count
    image = pl.pallas_call(
        place_kernel,
        out_shape=jax.ShapeDtypeStruct((2 * pol_count, beams, range_dev), jnp.bfloat16),
        in_specs=[vmem],
        out_specs=vmem,
        scratch_shapes=[
            pltpu.VMEM((total_slots * 32, range_dev // RBLOCK * beams), jnp.bfloat16),
            pltpu.VMEM((total_slots * 32, 8 * RBLOCK), jnp.bfloat16),
        ],
        compiler_params=pltpu.CompilerParams(vmem_limit_bytes=56 << 20),
    )(gathered)
    return image.reshape(2, pol_count, beams, range_dev)


def solution(mesh):
    placed = (
        P(None, "pulse", None, "tile"),
        P(),
        P(),
        P(),
        P(),
        P(),
        P("pulse", "tile"),
        P("pulse", "tile"),
        P("pulse", "tile", None),
        P("pulse", "tile", None),
    )
    return jax.shard_map(
        shards,
        mesh=mesh,
        in_specs=placed,
        out_specs=P(None, None, "pulse", "tile"),
        check_vma=False,
    )
```

```python
import functools
import math

import jax
import jax.numpy as jnp
from jax import lax
from jax.experimental import pallas as pl
from jax.experimental.pallas import tpu as pltpu
from jax.sharding import PartitionSpec as P

RBLOCK = 128
CAP = 2
CBLOCK = 256
EDGE = 128
TABROWS = 16


def shifted(value, axis, by):
    count = lax.axis_size(axis)
    pairs = [(i, i + by) for i in range(count) if 0 <= i + by < count]
    return lax.ppermute(value, axis, pairs)


def iota(shape, dim):
    return lax.broadcasted_iota(jnp.int32, shape, dim)


def form_kernel(
    shift_ref, coef_ref, foot_ref, slot_ref,
    own_ref, next_ref, prev_ref, after_ref, replica_ref, steer_ref, index_ref, frac_ref,
    kid_ref, tab_ref,
    ext_ref, toep_ref, sub_ref, merged_ref,
):
    range_dev = own_ref.shape[2]
    rows = own_ref.shape[1]
    taps = replica_ref.shape[1]
    window = CBLOCK + taps
    width = sub_ref.shape[1]
    blocks = range_dev // RBLOCK
    bf16 = jnp.bfloat16

    ext_ref[:, :, 0:EDGE] = prev_ref[...]
    ext_ref[:, :, EDGE : EDGE + range_dev] = own_ref[...]
    ext_ref[:, :, EDGE + range_dev : EDGE + 2 * range_dev] = next_ref[...]
    ext_ref[:, :, EDGE + 2 * range_dev :] = after_ref[...]

    for part in range(2):
        line = replica_ref[part : part + 1, :].astype(jnp.float32)
        line = jnp.concatenate([line, jnp.zeros((1, CBLOCK), jnp.float32)], axis=1)
        rolled = pltpu.roll(
            jnp.broadcast_to(line, (CBLOCK, window)), 0, 1, stride=1, stride_axis=0
        )
        if part == 0:
            toep_ref[0:CBLOCK, 0:window] = rolled.astype(bf16)
            toep_ref[CBLOCK:, window:] = rolled.astype(bf16)
        else:
            toep_ref[0:CBLOCK, window:] = rolled.astype(bf16)
            toep_ref[CBLOCK:, 0:window] = (-rolled).astype(bf16)

    r_at = iota((256, 32), 0)
    left = (((r_at >> 2) & 1) * 16 + ((r_at >> 3) & 15) == iota((256, 32), 1)).astype(bf16)
    k_at = iota((32, 256), 1)
    right = ((k_at >> 7) * 16 + ((k_at >> 2) & 15) == iota((32, 256), 0)).astype(bf16)
    spread = jnp.dot(left, steer_ref[...], preferred_element_type=jnp.float32).astype(bf16)
    spread = jnp.dot(spread, right, preferred_element_type=jnp.float32)
    r_all, k_all = iota((256, 256), 0), iota((256, 256), 1)
    same = ((r_all >> 7) == ((k_all >> 6) & 1)) & ((r_all & 3) == (k_all & 3))
    steer = jnp.where(same, spread, 0.0).astype(bf16)

    group = 3

    def compress(at, carry):
        pieces = []
        for step in range(group):
            start = pl.multiple_of((at * group + step) * CBLOCK, CBLOCK)
            pieces.append(
                jnp.concatenate(
                    [ext_ref[0, :, pl.ds(start, window)], ext_ref[1, :, pl.ds(start, window)]],
                    axis=1,
                )
            )
        left_side = jnp.concatenate(pieces, axis=0)
        found = lax.dot_general(
            left_side, toep_ref[...], (((1,), (1,)), ((), ())),
            preferred_element_type=jnp.float32,
        ).astype(bf16)
        for step in range(group):
            start = pl.multiple_of((at * group + step) * CBLOCK, CBLOCK)
            one = found[step * rows : (step + 1) * rows]
            stacked = jnp.concatenate([one[:, :CBLOCK], one[:, CBLOCK:]], axis=0)
            sub = jnp.dot(steer, stacked, preferred_element_type=jnp.float32)
            sub_ref[:, pl.ds(start, CBLOCK)] = sub.astype(bf16).astype(jnp.float32)
        return carry

    lax.fori_loop(0, width // (CBLOCK * group), compress, 0)

    @pl.when(lax.axis_index("tile") == 0)
    def _():
        sub_ref[:, 0:EDGE] = jnp.zeros((256, EDGE), jnp.float32)

    sign = jnp.where(iota((8, width), 0) < 4, -1.0, 1.0).astype(jnp.float32)

    def merge(a, carry):
        totals = [None, None]
        for c in range(2):
            x = sub_ref[pl.ds(pl.multiple_of((c * 16 + a) * 8, 8), 8), :]
            x_up = pltpu.roll(x, width - 1, 1)
            for parity in range(2):
                b = 2 * a + parity
                weight = coef_ref[0, c * 32 + b]
                cosine = coef_ref[1, c * 32 + b]
                sine = coef_ref[2, c * 32 + b]
                y = (1.0 - weight) * x + weight * x_up
                v = cosine * y + (sine * sign) * pltpu.roll(y, 4, 0)
                by = shift_ref[c, b]
                z = pltpu.roll(v, jnp.where(by > 0, width - by, -by), 1)
                z = z[:, EDGE : EDGE + range_dev]
                totals[parity] = z if totals[parity] is None else totals[parity] + z
        merged_ref[pl.ds(pl.multiple_of(a * 16, 16), 16), :] = jnp.concatenate(
            totals, axis=0
        ).astype(bf16)
        return carry

    lax.fori_loop(0, 16, merge, 0)

    order = (k_all == (r_all & 31) * 8 + (r_all >> 5)).astype(bf16)
    if tab_ref.shape[0] > blocks:
        kid_ref[...] = jnp.zeros(kid_ref.shape, bf16)
        tab_ref[...] = jnp.zeros(tab_ref.shape, bf16)
    tab_row = iota((TABROWS, RBLOCK), 0)
    for f in range(blocks):
        foot = foot_ref[0, f]
        rank = jnp.int32(0)
        for before in range(f):
            rank = rank + (foot_ref[0, before] == foot).astype(jnp.int32)
        slot = foot * CAP + rank
        part = jnp.dot(
            order, merged_ref[:, f * RBLOCK : (f + 1) * RBLOCK],
            preferred_element_type=jnp.float32,
        )
        kid_ref[:, slot] = part.astype(bf16).reshape(8, 32, RBLOCK)
        landing = (slot_ref[0, f] + 1).astype(jnp.float32)
        index_f = index_ref[0, f : f + 1, :].astype(jnp.float32)
        frac_f = frac_ref[0, f : f + 1, :].astype(jnp.float32)
        table = jnp.where(tab_row == 0, index_f, jnp.where(tab_row == 1, frac_f, 0.0))
        table = jnp.where(tab_row == 2, landing, table)
        tab_ref[slot] = table.astype(bf16)


def place_kernel(got_ref, out_ref, left_ref, right_ref):
    slots = got_ref.shape[0]
    beams = out_ref.shape[1]
    spans = out_ref.shape[2] // RBLOCK
    lanes = spans * beams
    mine = lax.axis_index("pulse") * beams
    bf16 = jnp.bfloat16
    lane = iota((RBLOCK, lanes), 1)
    widen = ((lane & (beams - 1)) + mine == iota((RBLOCK, lanes), 0)).astype(bf16)
    where_at = iota((1, lanes), 1) // beams + 1
    child = iota((32, lanes), 0).astype(jnp.float32)

    def prepare(at, carry):
        table = got_ref[at, 256 : 256 + TABROWS, :]
        wide = jnp.dot(table, widen, preferred_element_type=jnp.float32)
        landing = wide[2:3, :]
        index = jnp.where(landing == where_at.astype(jnp.float32), wide[0:1, :], -9.0)
        frac = wide[1:2, :]
        lower = (1.0 - frac).astype(bf16).astype(jnp.float32)
        weight = jnp.where(child == index, lower, 0.0)
        weight = jnp.where(child == index + 1.0, frac, weight)
        start = pl.multiple_of(at * 32, 32)
        left_ref[pl.ds(start, 32), :] = weight.astype(bf16)
        for x in range(8):
            right_ref[pl.ds(start, 32), x * RBLOCK : (x + 1) * RBLOCK] = got_ref[
                at, x * 32 : (x + 1) * 32, :
            ]
        return carry

    lax.fori_loop(0, slots, prepare, 0)
    for half in range(0, lanes, 256):
        result = lax.dot_general(
            left_ref[:, half : half + 256], right_ref[...], (((0,), (0,)), ((), ())),
            preferred_element_type=jnp.float32,
        ).astype(bf16)
        for sub in range(256 // beams):
            w = half // beams + sub
            for x in range(8):
                out_ref[x, :, w * RBLOCK : (w + 1) * RBLOCK] = result[
                    sub * beams : (sub + 1) * beams, x * RBLOCK : (x + 1) * RBLOCK
                ]


CHUNKS = 4
MESH = pl.DeviceIdType.MESH


STAGES = 2


def fused_kernel(
    tiles, shift_ref, coef_ref, foot_ref,
    echo_ref, replica_ref, steer_ref, table_ref, out_ref,
    ext_ref, toep_ref, sub_ref, merged_ref, block_ref, kid_ref, tab_ref,
    kids, tabs, packed_ref, left_ref, part_ref, arrived_ref, own_ref,
    halo_send, halo_recv,
    a2a_send, a2a_recv, line_send, line_recv, part_send, part_recv,
):
    g = lax.axis_index("pulse")
    t = lax.axis_index("tile")
    beams = out_ref.shape[1]
    spans = out_ref.shape[2] // RBLOCK
    lanes = spans * beams
    slots = tiles * CAP
    depth = slots * 32
    per = 8 // CHUNKS
    bf16 = jnp.bfloat16
    f32 = jnp.float32
    is_mid = (g == 1) | (g == 2)
    inner = jnp.where(g == 0, 1, jnp.where(g == 1, 2, jnp.where(g == 2, 1, 2)))
    end = jnp.where(g < 2, 0, 3)
    far = 3 - end

    barrier = pltpu.get_barrier_semaphore()
    for d in range(1, tiles):
        pl.semaphore_signal(
            barrier, inc=1, device_id={"tile": lax.rem(t + d, tiles)}, device_id_type=MESH
        )
    pl.semaphore_signal(barrier, inc=1, device_id={"pulse": inner}, device_id_type=MESH)

    @pl.when(is_mid)
    def _():
        pl.semaphore_signal(barrier, inc=1, device_id={"pulse": end}, device_id_type=MESH)
        pl.semaphore_wait(barrier, tiles + 1)

    @pl.when(jnp.logical_not(is_mid))
    def _():
        pl.semaphore_wait(barrier, tiles)

    range_dev = echo_ref.shape[3]
    rows = echo_ref.shape[2]
    taps = replica_ref.shape[1]
    window = CBLOCK + taps
    width = sub_ref.shape[1]
    blocks = range_dev // RBLOCK

    halos = [
        ((0, range_dev), EDGE + range_dev, -1),
        ((range_dev - EDGE, EDGE), 0, 1),
        ((0, EDGE), EDGE + 2 * range_dev, -2),
    ]

    def halo_copy(stage, j):
        (first, count), to, by = halos[j]
        return pltpu.make_async_remote_copy(
            src_ref=echo_ref.at[stage, :, :, pl.ds(first, count)],
            dst_ref=ext_ref.at[stage, :, :, pl.ds(to, count)],
            send_sem=halo_send.at[stage, j], recv_sem=halo_recv.at[stage, j],
            device_id={"tile": lax.rem(t + by + tiles, tiles)}, device_id_type=MESH,
        )

    def sends(j):
        by = halos[j][2]
        return (t + by >= 0) & (t + by < tiles)

    def gets(j):
        by = halos[j][2]
        return (t - by >= 0) & (t - by < tiles)

    for stage in range(STAGES):
        for j in range(3):
            @pl.when(sends(j))
            def _():
                halo_copy(stage, j).start()

    for stage in range(STAGES):
        for j in range(3):
            (_, count), to, _ = halos[j]

            @pl.when(jnp.logical_not(gets(j)))
            def _():
                ext_ref[stage, :, :, to : to + count] = jnp.zeros((2, rows, count), bf16)

        ext_ref[stage, :, :, EDGE : EDGE + range_dev] = echo_ref[stage]

    for part in range(2):
        line = replica_ref[part : part + 1, :].astype(f32)
        line = jnp.concatenate([line, jnp.zeros((1, CBLOCK), f32)], axis=1)
        rolled = pltpu.roll(
            jnp.broadcast_to(line, (CBLOCK, window)), 0, 1, stride=1, stride_axis=0
        )
        if part == 0:
            toep_ref[0:CBLOCK, 0:window] = rolled.astype(bf16)
            toep_ref[CBLOCK:, window:] = rolled.astype(bf16)
        else:
            toep_ref[0:CBLOCK, window:] = rolled.astype(bf16)
            toep_ref[CBLOCK:, 0:window] = (-rolled).astype(bf16)

    r_at = iota((256, 32), 0)
    turn, want = (r_at >> 2) & 1, (r_at >> 1) & 1
    picked = jnp.where(turn == 1, 1 - want, want)
    left = ((picked * 16 + ((r_at >> 3) & 15)) == iota((256, 32), 1)).astype(f32)
    left = jnp.where((turn == 1) & (want == 0), -left, left).astype(bf16)
    k_at = iota((32, 128), 1)
    right = ((k_at >> 6) * 16 + ((k_at >> 1) & 15) == iota((32, 128), 0)).astype(bf16)
    spread = jnp.dot(left, steer_ref[...], preferred_element_type=f32).astype(bf16)
    spread = jnp.dot(spread, right, preferred_element_type=f32)
    r_all, k_all = iota((256, 128), 0), iota((256, 128), 1)
    same = ((r_all >> 7) == ((k_all >> 5) & 1)) & ((r_all & 1) == (k_all & 1))
    steer = jnp.where(same, spread, 0.0).astype(bf16)
    o_all, i_all = iota((128, 128), 0), iota((128, 128), 1)
    order_in = (o_all & 31) * 4 + ((o_all >> 5) & 1) * 2 + (o_all >> 6)
    reorder = (i_all == order_in).astype(bf16)

    targets = []
    for f in range(blocks):
        rank = jnp.int32(0)
        for earlier in range(f):
            rank = rank + (foot_ref[0, earlier] == foot_ref[0, f]).astype(jnp.int32)
        targets.append(foot_ref[0, f] * CAP + rank)
    sources = []
    for s in range(slots):
        source = jnp.int32(0)
        for f in range(blocks):
            source = source + f * (targets[f] == s).astype(jnp.int32)
        sources.append(source)
    for s in range(slots):
        tab_ref[s] = table_ref[sources[s]]

    group = 3

    def form(stage, between):
        for j in range(3):
            @pl.when(gets(j))
            def _():
                halo_copy(stage, j).wait_recv()

        def compress(at, carry):
            pieces = []
            for step in range(group):
                start = pl.multiple_of((at * group + step) * CBLOCK, CBLOCK)
                pieces.append(
                    jnp.concatenate(
                        [
                            ext_ref[stage, 0, :, pl.ds(start, window)],
                            ext_ref[stage, 1, :, pl.ds(start, window)],
                        ],
                        axis=1,
                    )
                )
            found = lax.dot_general(
                jnp.concatenate(pieces, axis=0), toep_ref[...], (((1,), (1,)), ((), ())),
                preferred_element_type=f32,
            ).astype(bf16)
            for step in range(group):
                start = pl.multiple_of((at * group + step) * CBLOCK, CBLOCK)
                one = found[step * rows : (step + 1) * rows]
                stacked = jnp.concatenate([one[:, :CBLOCK], one[:, CBLOCK:]], axis=0)
                sub = jnp.dot(steer, stacked, preferred_element_type=f32)
                sub_ref[:, pl.ds(start, CBLOCK)] = sub.astype(bf16).astype(f32)
            return carry

        lax.fori_loop(0, width // (CBLOCK * group), compress, 0)

        @pl.when(t == 0)
        def _():
            sub_ref[:, 0:EDGE] = jnp.zeros((256, EDGE), f32)

        between()

        def merge(a, carry):
            totals = [None, None]
            for c in range(2):
                x = sub_ref[pl.ds(pl.multiple_of((c * 16 + a) * 8, 8), 8), :]
                x_up = pltpu.roll(x, width - 1, 1)
                for parity in range(2):
                    b = 2 * a + parity
                    weight = coef_ref[0, c * 32 + b]
                    cosine = coef_ref[1, c * 32 + b]
                    sine = coef_ref[2, c * 32 + b]
                    y = (1.0 - weight) * x + weight * x_up
                    v = cosine * y + sine * pltpu.roll(y, 4, 0)
                    by = shift_ref[c, b]
                    z = pltpu.roll(v, jnp.where(by > 0, width - by, -by), 1)
                    z = z[:, EDGE : EDGE + range_dev]
                    totals[parity] = z if totals[parity] is None else totals[parity] + z
            both = jnp.where(
                iota((8, range_dev), 0) < 4, totals[0], pltpu.roll(totals[1], 4, 0)
            )
            merged_ref[pl.ds(pl.multiple_of(a * 8, 8), 8), :] = both
            return carry

        lax.fori_loop(0, 16, merge, 0)
        for f in range(blocks):
            part = jnp.dot(
                reorder, merged_ref[:, f * RBLOCK : (f + 1) * RBLOCK].astype(bf16),
                preferred_element_type=f32,
            )
            block_ref[f] = part.astype(bf16).reshape(4, 32, RBLOCK)
        for s in range(slots):
            kid_ref[stage * 4 : stage * 4 + 4, s] = block_ref[sources[s]]

    def spread_copy(k, d, peer, place):
        if k == CHUNKS:
            src = tab_ref.at[pl.ds(peer * CAP, CAP)]
            dst = tabs.at[pl.ds(place * CAP, CAP)]
        else:
            src = kid_ref.at[pl.ds(k * per, per), pl.ds(peer * CAP, CAP)]
            dst = kids.at[g, pl.ds(k * per, per), pl.ds(place * CAP, CAP)]
        return pltpu.make_async_remote_copy(
            src_ref=src, dst_ref=dst,
            send_sem=a2a_send.at[k, d - 1], recv_sem=a2a_recv.at[k, d - 1],
            device_id={"tile": peer}, device_id_type=MESH,
        )

    order = [CHUNKS] + list(range(CHUNKS))

    def spread_start(k):
        for d in range(1, tiles):
            spread_copy(k, d, lax.rem(t + d, tiles), t).start()

    def spread_wait(k):
        for d in range(1, tiles):
            peer = lax.rem(t + tiles - d, tiles)
            spread_copy(k, d, peer, peer).wait_recv()

    def line_copy(k, group, lane, to):
        if k == CHUNKS:
            part = packed_ref.at[group]
        else:
            part = kids.at[group, pl.ds(k * per, per)]
        return pltpu.make_async_remote_copy(
            src_ref=part, dst_ref=part,
            send_sem=line_send.at[lane, k], recv_sem=line_recv.at[group, k],
            device_id={"pulse": to}, device_id_type=MESH,
        )

    middle = spans // 2 * RBLOCK

    def part_copy(k, half, to):
        return pltpu.make_async_remote_copy(
            src_ref=part_ref.at[pl.ds(k * per, per), :, pl.ds(half * middle, middle)],
            dst_ref=arrived_ref.at[pl.ds(k * per, per), :, pl.ds(half * middle, middle)],
            send_sem=part_send.at[k, half], recv_sem=part_recv.at[k, half],
            device_id={"pulse": to}, device_id_type=MESH,
        )

    def prepare(group, beam_group, row, column, used):
        expand = (
            (iota((RBLOCK, lanes), 1) & (beams - 1)) + beam_group * beams
            == iota((RBLOCK, lanes), 0)
        ).astype(bf16)
        where_at = (iota((1, lanes), 1) // beams + 1).astype(f32)
        child = iota((32, lanes), 0).astype(f32)

        wide = jnp.dot(packed_ref[group], expand, preferred_element_type=f32)
        for at in range(slots // 4):
            pieces = []
            for slot in range(at * 4, at * 4 + 4):
                landing = wide[2 * slots + slot : 2 * slots + slot + 1, :]
                index = jnp.where(
                    (landing == where_at) & used, wide[slot : slot + 1, :], -9.0
                )
                frac = wide[slots + slot : slots + slot + 1, :]
                lower = (1.0 - frac).astype(bf16).astype(f32)
                weight = jnp.where(child == index, lower, 0.0)
                pieces.append(jnp.where(child == index + 1.0, frac, weight))
            block = jnp.concatenate(pieces, axis=0)
            at_column = pl.multiple_of(column + at * 128, 128)
            left_ref[row : row + lanes, pl.ds(at_column, 128)] = block.T.astype(bf16)

    def keep(k):
        if k == CHUNKS:
            tabs[pl.ds(t * CAP, CAP)] = tab_ref[pl.ds(t * CAP, CAP)]
        else:
            span = slice(k * per, (k + 1) * per)
            kids[g, span, pl.ds(t * CAP, CAP)] = kid_ref[span, pl.ds(t * CAP, CAP)]

    def begin_own(k):
        spread_wait(k)
        if k == CHUNKS:
            row, column = iota((3 * slots, slots * TABROWS), 0), iota((3 * slots, slots * TABROWS), 1)
            choose = column == (row & (slots - 1)) * TABROWS + row // slots
            packed_ref[g] = jnp.dot(
                choose.astype(bf16), tabs[...].reshape(slots * TABROWS, RBLOCK),
                preferred_element_type=f32,
            ).astype(bf16)
        line_copy(k, g, 0, inner).start()

    spread_start(CHUNKS)
    keep(CHUNKS)
    form(0, lambda: begin_own(CHUNKS))
    for k in (0, 1):
        spread_start(k)
        keep(k)

    def between():
        begin_own(0)
        begin_own(1)

    form(1, between)
    for k in (2, 3):
        spread_start(k)
        keep(k)

    @pl.when(is_mid)
    def _():
        def relay(k):
            line_copy(k, end, 0, inner).wait_recv()
            line_copy(k, end, 1, inner).start()

        def finish(k):
            line_copy(k, inner, 0, inner).wait_recv()
            line_copy(k, far, 0, inner).wait_recv()

        relay(CHUNKS)
        relay(0)
        finish(CHUNKS)

        def prepare_group(group, carry):
            column = pl.multiple_of(group * depth, 128)
            prepare(group, g, 0, column, group >= 0)
            prepare(group, end, lanes, column, group != end)
            return carry

        lax.fori_loop(0, 4, prepare_group, 0)
        relay(1)
        begin_own(2)
        begin_own(3)
        for k in range(CHUNKS):
            if 2 <= k + 1 < CHUNKS:
                relay(k + 1)
            finish(k)
            right = jnp.concatenate(
                [kids[:, k * per + i].reshape(4 * depth, RBLOCK) for i in range(per)], axis=1
            )
            for half in range(2):
                first = lanes + half * (lanes // 2)
                result = jnp.dot(
                    left_ref[first : first + lanes // 2, :], right, preferred_element_type=f32
                ).astype(bf16)
                for step in range(spans // 2):
                    w = half * (spans // 2) + step
                    for i in range(per):
                        part_ref[k * per + i, :, w * RBLOCK : (w + 1) * RBLOCK] = result[
                            step * beams : (step + 1) * beams, i * RBLOCK : (i + 1) * RBLOCK
                        ]
                part_copy(k, half, end).start()
            result = jnp.dot(
                left_ref[:lanes, :], right, preferred_element_type=f32
            ).astype(bf16)
            for w in range(spans):
                for i in range(per):
                    out_ref[i * 4 + k, :, w * RBLOCK : (w + 1) * RBLOCK] = result[
                        w * beams : (w + 1) * beams, i * RBLOCK : (i + 1) * RBLOCK
                    ]
        for k in order:
            line_copy(k, g, 0, inner).wait_send()
            line_copy(k, end, 1, inner).wait_send()
        for k in range(CHUNKS):
            for half in range(2):
                part_copy(k, half, end).wait_send()

    @pl.when(jnp.logical_not(is_mid))
    def _():
        begin_own(2)
        begin_own(3)
        prepare(g, g, 0, 0, g >= 0)
        for k in range(CHUNKS):
            right = jnp.concatenate(
                [kids[g, k * per + i].reshape(depth, RBLOCK) for i in range(per)], axis=1
            )
            result = jnp.dot(
                left_ref[:lanes, :depth], right, preferred_element_type=f32
            )
            for w in range(spans):
                for i in range(per):
                    own_ref[k * per + i, :, w * RBLOCK : (w + 1) * RBLOCK] = result[
                        w * beams : (w + 1) * beams, i * RBLOCK : (i + 1) * RBLOCK
                    ]
        for k in range(CHUNKS):
            for half in range(2):
                part_copy(k, half, inner).wait_recv()
                span = slice(half * middle, (half + 1) * middle)
                for i in range(per):
                    x = k * per + i
                    out_ref[i * 4 + k, :, span] = (
                        own_ref[x, :, span] + arrived_ref[x, :, span].astype(f32)
                    ).astype(bf16)
        for k in order:
            line_copy(k, g, 0, inner).wait_send()

    for k in order:
        for d in range(1, tiles):
            spread_copy(k, d, lax.rem(t + d, tiles), t).wait_send()
    for stage in range(STAGES):
        for j in range(3):
            @pl.when(sends(j))
            def _():
                halo_copy(stage, j).wait_send()


def fused(shift, coef, foot, echoes, replica, steer, tables, tiles, beams, range_dev):
    slots = tiles * CAP
    lanes = range_dev // RBLOCK * beams
    bf16 = jnp.bfloat16
    vmem = pl.BlockSpec(memory_space=pltpu.VMEM)
    smem = pl.BlockSpec(memory_space=pltpu.SMEM)
    dma = pltpu.SemaphoreType.DMA
    return pl.pallas_call(
        functools.partial(fused_kernel, tiles),
        out_shape=jax.ShapeDtypeStruct((8, beams, range_dev), bf16),
        in_specs=[smem] * 3 + [vmem] * 4,
        out_specs=vmem,
        scratch_shapes=[
            pltpu.VMEM(echoes.shape[:3] + (2 * range_dev + 2 * EDGE,), bf16),
            pltpu.VMEM((2 * CBLOCK, 2 * (CBLOCK + replica.shape[1])), bf16),
            pltpu.VMEM((256, range_dev + CBLOCK), jnp.float32),
            pltpu.VMEM((128, range_dev), jnp.float32),
            pltpu.VMEM((slots, 4, 32, RBLOCK), bf16),
            pltpu.VMEM((8, slots, 32, RBLOCK), bf16),
            pltpu.VMEM((slots, TABROWS, RBLOCK), bf16),
            pltpu.VMEM((4, 8, slots, 32, RBLOCK), bf16),
            pltpu.VMEM((slots, TABROWS, RBLOCK), bf16),
            pltpu.VMEM((4, 3 * slots, RBLOCK), bf16),
            pltpu.VMEM((2 * lanes, 4 * slots * 32), bf16),
            pltpu.VMEM((8, beams, range_dev), bf16),
            pltpu.VMEM((8, beams, range_dev), bf16),
            pltpu.VMEM((8, beams, range_dev), jnp.float32),
            dma((STAGES, 3)),
            dma((STAGES, 3)),
            dma((CHUNKS + 1, tiles - 1)),
            dma((CHUNKS + 1, tiles - 1)),
            dma((2, CHUNKS + 1)),
            dma((4, CHUNKS + 1)),
            dma((CHUNKS, 2)),
            dma((CHUNKS, 2)),
        ],
        compiler_params=pltpu.CompilerParams(
            collective_id=0, has_side_effects=True, vmem_limit_bytes=56 << 20
        ),
    )(shift, coef, foot, echoes, replica, steer, tables)


def shards(
    echoes, replica, steer_phase, range_shift, merge_phase, merge_frac,
    footprint, row_slot, beam_index, beam_frac,
):
    pulse_count, pol_count, range_dev = echoes.shape[1:]
    rows = pulse_count * pol_count
    taps = replica.shape[1]
    final_beams = beam_index.shape[2]
    tiles = lax.axis_size("tile")
    groups = lax.axis_size("pulse")
    slot_count = tiles * CAP
    scale = 1.0 / math.sqrt(steer_phase.shape[1])
    steer_re = jnp.cos(steer_phase) * scale
    steer_im = jnp.sin(steer_phase) * scale
    steer = jnp.concatenate(
        [
            jnp.concatenate([steer_re, -steer_im], axis=1),
            jnp.concatenate([steer_im, steer_re], axis=1),
        ],
        axis=0,
    ).astype(jnp.bfloat16)
    half_root = math.sqrt(0.5)
    coef = jnp.stack(
        [
            merge_frac.reshape(-1),
            (jnp.cos(merge_phase) * half_root).reshape(-1),
            (jnp.sin(merge_phase) * half_root).reshape(-1),
        ]
    )
    beams = final_beams // groups
    if groups == 4 and slot_count == range_dev // RBLOCK:
        split = echoes.reshape(2, pulse_count, STAGES, pol_count // STAGES, range_dev)
        split = split.transpose(2, 0, 1, 3, 4).reshape(STAGES, 2, rows // STAGES, range_dev)
        landing = jnp.broadcast_to(row_slot[0][:, None] + 1, beam_index.shape[1:])
        tables = jnp.stack(
            [beam_index[0].astype(jnp.float32), beam_frac[0].astype(jnp.float32),
             landing.astype(jnp.float32)], axis=1,
        )
        tables = jnp.pad(tables, ((0, 0), (0, TABROWS - 3), (0, 0))).astype(jnp.bfloat16)
        image = fused(
            range_shift, coef, footprint, split, replica, steer, tables,
            tiles, beams, range_dev,
        )
        return image.reshape(2, pol_count, beams, range_dev)
    own = echoes.reshape(2, rows, range_dev)
    following = shifted(own, "tile", -1)
    before = shifted(own[:, :, range_dev - EDGE :], "tile", 1)
    after = shifted(own[:, :, :EDGE], "tile", -2)

    width = range_dev + CBLOCK
    smem = pl.BlockSpec(memory_space=pltpu.SMEM)
    vmem = pl.BlockSpec(memory_space=pltpu.VMEM)
    kids, tabs = pl.pallas_call(
        form_kernel,
        out_shape=(
            jax.ShapeDtypeStruct((8, slot_count, 32, RBLOCK), jnp.bfloat16),
            jax.ShapeDtypeStruct((slot_count, TABROWS, RBLOCK), jnp.bfloat16),
        ),
        in_specs=[smem] * 4 + [vmem] * 8,
        out_specs=(vmem, vmem),
        scratch_shapes=[
            pltpu.VMEM((2, rows, 2 * range_dev + 2 * EDGE), jnp.bfloat16),
            pltpu.VMEM((2 * CBLOCK, 2 * (CBLOCK + taps)), jnp.bfloat16),
            pltpu.VMEM((256, width), jnp.float32),
            pltpu.VMEM((256, range_dev), jnp.bfloat16),
        ],
        compiler_params=pltpu.CompilerParams(vmem_limit_bytes=56 << 20),
    )(
        range_shift, coef, footprint, row_slot,
        own, following, before, after, replica, steer, beam_index, beam_frac,
    )
    sent = jnp.concatenate(
        [kids.transpose(1, 0, 2, 3).reshape(slot_count, 256, RBLOCK), tabs], axis=1
    )
    got = lax.all_to_all(
        sent.reshape(tiles, CAP, 256 + TABROWS, RBLOCK), "tile",
        split_axis=0, concat_axis=0, tiled=True,
    ).reshape(slot_count, 256 + TABROWS, RBLOCK)
    gathered = lax.all_gather(got, "pulse", axis=0, tiled=True)
    total_slots = groups * slot_count
    image = pl.pallas_call(
        place_kernel,
        out_shape=jax.ShapeDtypeStruct((2 * pol_count, beams, range_dev), jnp.bfloat16),
        in_specs=[vmem],
        out_specs=vmem,
        scratch_shapes=[
            pltpu.VMEM((total_slots * 32, range_dev // RBLOCK * beams), jnp.bfloat16),
            pltpu.VMEM((total_slots * 32, 8 * RBLOCK), jnp.bfloat16),
        ],
        compiler_params=pltpu.CompilerParams(vmem_limit_bytes=56 << 20),
    )(gathered)
    return image.reshape(2, pol_count, beams, range_dev)


def solution(mesh):
    placed = (
        P(None, "pulse", None, "tile"),
        P(),
        P(),
        P(),
        P(),
        P(),
        P("pulse", "tile"),
        P("pulse", "tile"),
        P("pulse", "tile", None),
        P("pulse", "tile", None),
    )
    return jax.shard_map(
        shards,
        mesh=mesh,
        in_specs=placed,
        out_specs=P(None, None, "pulse", "tile"),
        check_vma=False,
    )
```

```python
import functools
import math

import jax
import jax.numpy as jnp
from jax import lax
from jax.experimental import pallas as pl
from jax.experimental.pallas import tpu as pltpu
from jax.sharding import PartitionSpec as P

RBLOCK = 128
CAP = 2
CBLOCK = 256
EDGE = 128
TABROWS = 16


def shifted(value, axis, by):
    count = lax.axis_size(axis)
    pairs = [(i, i + by) for i in range(count) if 0 <= i + by < count]
    return lax.ppermute(value, axis, pairs)


def iota(shape, dim):
    return lax.broadcasted_iota(jnp.int32, shape, dim)


def form_kernel(
    shift_ref, coef_ref, foot_ref, slot_ref,
    own_ref, next_ref, prev_ref, after_ref, replica_ref, steer_ref, index_ref, frac_ref,
    kid_ref, tab_ref,
    ext_ref, toep_ref, sub_ref, merged_ref,
):
    range_dev = own_ref.shape[2]
    rows = own_ref.shape[1]
    taps = replica_ref.shape[1]
    window = CBLOCK + taps
    width = sub_ref.shape[1]
    blocks = range_dev // RBLOCK
    bf16 = jnp.bfloat16

    ext_ref[:, :, 0:EDGE] = prev_ref[...]
    ext_ref[:, :, EDGE : EDGE + range_dev] = own_ref[...]
    ext_ref[:, :, EDGE + range_dev : EDGE + 2 * range_dev] = next_ref[...]
    ext_ref[:, :, EDGE + 2 * range_dev :] = after_ref[...]

    for part in range(2):
        line = replica_ref[part : part + 1, :].astype(jnp.float32)
        line = jnp.concatenate([line, jnp.zeros((1, CBLOCK), jnp.float32)], axis=1)
        rolled = pltpu.roll(
            jnp.broadcast_to(line, (CBLOCK, window)), 0, 1, stride=1, stride_axis=0
        )
        if part == 0:
            toep_ref[0:CBLOCK, 0:window] = rolled.astype(bf16)
            toep_ref[CBLOCK:, window:] = rolled.astype(bf16)
        else:
            toep_ref[0:CBLOCK, window:] = rolled.astype(bf16)
            toep_ref[CBLOCK:, 0:window] = (-rolled).astype(bf16)

    r_at = iota((256, 32), 0)
    left = (((r_at >> 2) & 1) * 16 + ((r_at >> 3) & 15) == iota((256, 32), 1)).astype(bf16)
    k_at = iota((32, 256), 1)
    right = ((k_at >> 7) * 16 + ((k_at >> 2) & 15) == iota((32, 256), 0)).astype(bf16)
    spread = jnp.dot(left, steer_ref[...], preferred_element_type=jnp.float32).astype(bf16)
    spread = jnp.dot(spread, right, preferred_element_type=jnp.float32)
    r_all, k_all = iota((256, 256), 0), iota((256, 256), 1)
    same = ((r_all >> 7) == ((k_all >> 6) & 1)) & ((r_all & 3) == (k_all & 3))
    steer = jnp.where(same, spread, 0.0).astype(bf16)

    group = 3

    def compress(at, carry):
        pieces = []
        for step in range(group):
            start = pl.multiple_of((at * group + step) * CBLOCK, CBLOCK)
            pieces.append(
                jnp.concatenate(
                    [ext_ref[0, :, pl.ds(start, window)], ext_ref[1, :, pl.ds(start, window)]],
                    axis=1,
                )
            )
        left_side = jnp.concatenate(pieces, axis=0)
        found = lax.dot_general(
            left_side, toep_ref[...], (((1,), (1,)), ((), ())),
            preferred_element_type=jnp.float32,
        ).astype(bf16)
        for step in range(group):
            start = pl.multiple_of((at * group + step) * CBLOCK, CBLOCK)
            one = found[step * rows : (step + 1) * rows]
            stacked = jnp.concatenate([one[:, :CBLOCK], one[:, CBLOCK:]], axis=0)
            sub = jnp.dot(steer, stacked, preferred_element_type=jnp.float32)
            sub_ref[:, pl.ds(start, CBLOCK)] = sub.astype(bf16).astype(jnp.float32)
        return carry

    lax.fori_loop(0, width // (CBLOCK * group), compress, 0)

    @pl.when(lax.axis_index("tile") == 0)
    def _():
        sub_ref[:, 0:EDGE] = jnp.zeros((256, EDGE), jnp.float32)

    sign = jnp.where(iota((8, width), 0) < 4, -1.0, 1.0).astype(jnp.float32)

    def merge(a, carry):
        totals = [None, None]
        for c in range(2):
            x = sub_ref[pl.ds(pl.multiple_of((c * 16 + a) * 8, 8), 8), :]
            x_up = pltpu.roll(x, width - 1, 1)
            for parity in range(2):
                b = 2 * a + parity
                weight = coef_ref[0, c * 32 + b]
                cosine = coef_ref[1, c * 32 + b]
                sine = coef_ref[2, c * 32 + b]
                y = (1.0 - weight) * x + weight * x_up
                v = cosine * y + (sine * sign) * pltpu.roll(y, 4, 0)
                by = shift_ref[c, b]
                z = pltpu.roll(v, jnp.where(by > 0, width - by, -by), 1)
                z = z[:, EDGE : EDGE + range_dev]
                totals[parity] = z if totals[parity] is None else totals[parity] + z
        merged_ref[pl.ds(pl.multiple_of(a * 16, 16), 16), :] = jnp.concatenate(
            totals, axis=0
        ).astype(bf16)
        return carry

    lax.fori_loop(0, 16, merge, 0)

    order = (k_all == (r_all & 31) * 8 + (r_all >> 5)).astype(bf16)
    if tab_ref.shape[0] > blocks:
        kid_ref[...] = jnp.zeros(kid_ref.shape, bf16)
        tab_ref[...] = jnp.zeros(tab_ref.shape, bf16)
    tab_row = iota((TABROWS, RBLOCK), 0)
    for f in range(blocks):
        foot = foot_ref[0, f]
        rank = jnp.int32(0)
        for before in range(f):
            rank = rank + (foot_ref[0, before] == foot).astype(jnp.int32)
        slot = foot * CAP + rank
        part = jnp.dot(
            order, merged_ref[:, f * RBLOCK : (f + 1) * RBLOCK],
            preferred_element_type=jnp.float32,
        )
        kid_ref[:, slot] = part.astype(bf16).reshape(8, 32, RBLOCK)
        landing = (slot_ref[0, f] + 1).astype(jnp.float32)
        index_f = index_ref[0, f : f + 1, :].astype(jnp.float32)
        frac_f = frac_ref[0, f : f + 1, :].astype(jnp.float32)
        table = jnp.where(tab_row == 0, index_f, jnp.where(tab_row == 1, frac_f, 0.0))
        table = jnp.where(tab_row == 2, landing, table)
        tab_ref[slot] = table.astype(bf16)


def place_kernel(got_ref, out_ref, left_ref, right_ref):
    slots = got_ref.shape[0]
    beams = out_ref.shape[1]
    spans = out_ref.shape[2] // RBLOCK
    lanes = spans * beams
    mine = lax.axis_index("pulse") * beams
    bf16 = jnp.bfloat16
    lane = iota((RBLOCK, lanes), 1)
    widen = ((lane & (beams - 1)) + mine == iota((RBLOCK, lanes), 0)).astype(bf16)
    where_at = iota((1, lanes), 1) // beams + 1
    child = iota((32, lanes), 0).astype(jnp.float32)

    def prepare(at, carry):
        table = got_ref[at, 256 : 256 + TABROWS, :]
        wide = jnp.dot(table, widen, preferred_element_type=jnp.float32)
        landing = wide[2:3, :]
        index = jnp.where(landing == where_at.astype(jnp.float32), wide[0:1, :], -9.0)
        frac = wide[1:2, :]
        lower = (1.0 - frac).astype(bf16).astype(jnp.float32)
        weight = jnp.where(child == index, lower, 0.0)
        weight = jnp.where(child == index + 1.0, frac, weight)
        start = pl.multiple_of(at * 32, 32)
        left_ref[pl.ds(start, 32), :] = weight.astype(bf16)
        for x in range(8):
            right_ref[pl.ds(start, 32), x * RBLOCK : (x + 1) * RBLOCK] = got_ref[
                at, x * 32 : (x + 1) * 32, :
            ]
        return carry

    lax.fori_loop(0, slots, prepare, 0)
    for half in range(0, lanes, 256):
        result = lax.dot_general(
            left_ref[:, half : half + 256], right_ref[...], (((0,), (0,)), ((), ())),
            preferred_element_type=jnp.float32,
        ).astype(bf16)
        for sub in range(256 // beams):
            w = half // beams + sub
            for x in range(8):
                out_ref[x, :, w * RBLOCK : (w + 1) * RBLOCK] = result[
                    sub * beams : (sub + 1) * beams, x * RBLOCK : (x + 1) * RBLOCK
                ]


CHUNKS = 8
MESH = pl.DeviceIdType.MESH


STAGES = 2


def fused_kernel(
    tiles, shift_ref, coef_ref, foot_ref,
    echo_ref, replica_ref, steer_ref, table_ref, out_ref,
    ext_ref, toep_ref, sub_ref, merged_ref, block_ref, kid_ref, tab_ref,
    kids, tabs, packed_ref, left_ref, part_ref, arrived_ref, own_ref,
    halo_send, halo_recv,
    a2a_send, a2a_recv, line_send, line_recv, part_send, part_recv,
):
    g = lax.axis_index("pulse")
    t = lax.axis_index("tile")
    beams = out_ref.shape[1]
    spans = out_ref.shape[2] // RBLOCK
    lanes = spans * beams
    slots = tiles * CAP
    depth = slots * 32
    per = 8 // CHUNKS

    def out_at(x):
        return (x % 2) * 4 + x // 2

    bf16 = jnp.bfloat16
    f32 = jnp.float32
    is_mid = (g == 1) | (g == 2)
    inner = jnp.where(g == 0, 1, jnp.where(g == 1, 2, jnp.where(g == 2, 1, 2)))
    end = jnp.where(g < 2, 0, 3)
    far = 3 - end

    barrier = pltpu.get_barrier_semaphore()
    for d in range(1, tiles):
        pl.semaphore_signal(
            barrier, inc=1, device_id={"tile": lax.rem(t + d, tiles)}, device_id_type=MESH
        )
    pl.semaphore_signal(barrier, inc=1, device_id={"pulse": inner}, device_id_type=MESH)

    @pl.when(is_mid)
    def _():
        pl.semaphore_signal(barrier, inc=1, device_id={"pulse": end}, device_id_type=MESH)
        pl.semaphore_wait(barrier, tiles + 1)

    @pl.when(jnp.logical_not(is_mid))
    def _():
        pl.semaphore_wait(barrier, tiles)

    range_dev = echo_ref.shape[3]
    rows = echo_ref.shape[2]
    taps = replica_ref.shape[1]
    window = CBLOCK + taps
    width = sub_ref.shape[1]
    blocks = range_dev // RBLOCK

    halos = [
        ((0, range_dev), EDGE + range_dev, -1),
        ((range_dev - EDGE, EDGE), 0, 1),
        ((0, EDGE), EDGE + 2 * range_dev, -2),
    ]

    def halo_copy(stage, j):
        (first, count), to, by = halos[j]
        return pltpu.make_async_remote_copy(
            src_ref=echo_ref.at[:, stage, :, pl.ds(first, count)],
            dst_ref=ext_ref.at[stage, :, :, pl.ds(to, count)],
            send_sem=halo_send.at[stage, j], recv_sem=halo_recv.at[stage, j],
            device_id={"tile": lax.rem(t + by + tiles, tiles)}, device_id_type=MESH,
        )

    def sends(j):
        by = halos[j][2]
        return (t + by >= 0) & (t + by < tiles)

    def gets(j):
        by = halos[j][2]
        return (t - by >= 0) & (t - by < tiles)

    for stage in range(STAGES):
        for j in range(3):
            @pl.when(sends(j))
            def _():
                halo_copy(stage, j).start()

    for stage in range(STAGES):
        for j in range(3):
            (_, count), to, _ = halos[j]

            @pl.when(jnp.logical_not(gets(j)))
            def _():
                ext_ref[stage, :, :, to : to + count] = jnp.zeros((2, rows, count), bf16)

        ext_ref[stage, :, :, EDGE : EDGE + range_dev] = echo_ref[:, stage]

    for part in range(2):
        line = replica_ref[part : part + 1, :].astype(f32)
        line = jnp.concatenate([line, jnp.zeros((1, CBLOCK), f32)], axis=1)
        rolled = pltpu.roll(
            jnp.broadcast_to(line, (CBLOCK, window)), 0, 1, stride=1, stride_axis=0
        )
        if part == 0:
            toep_ref[0:CBLOCK, 0:window] = rolled.astype(bf16)
            toep_ref[CBLOCK:, window:] = rolled.astype(bf16)
        else:
            toep_ref[0:CBLOCK, window:] = rolled.astype(bf16)
            toep_ref[CBLOCK:, 0:window] = (-rolled).astype(bf16)

    r_at = iota((256, 32), 0)
    turn, want = (r_at >> 2) & 1, (r_at >> 1) & 1
    picked = jnp.where(turn == 1, 1 - want, want)
    left = ((picked * 16 + ((r_at >> 3) & 15)) == iota((256, 32), 1)).astype(f32)
    left = jnp.where((turn == 1) & (want == 0), -left, left).astype(bf16)
    k_at = iota((32, 128), 1)
    right = ((k_at >> 6) * 16 + (k_at & 15) == iota((32, 128), 0)).astype(bf16)
    spread = jnp.dot(left, steer_ref[...], preferred_element_type=f32).astype(bf16)
    spread = jnp.dot(spread, right, preferred_element_type=f32)
    r_all, k_all = iota((256, 128), 0), iota((256, 128), 1)
    same = ((r_all >> 7) == ((k_all >> 4) & 1)) & ((r_all & 1) == ((k_all >> 5) & 1))
    steer = jnp.where(same, spread, 0.0).astype(bf16)
    o_all, i_all = iota((128, 128), 0), iota((128, 128), 1)
    order_in = (o_all & 31) * 4 + ((o_all >> 5) & 1) * 2 + (o_all >> 6)
    reorder = (i_all == order_in).astype(bf16)

    targets = []
    for f in range(blocks):
        rank = jnp.int32(0)
        for earlier in range(f):
            rank = rank + (foot_ref[0, earlier] == foot_ref[0, f]).astype(jnp.int32)
        targets.append(foot_ref[0, f] * CAP + rank)
    sources = []
    for s in range(slots):
        source = jnp.int32(0)
        for f in range(blocks):
            source = source + f * (targets[f] == s).astype(jnp.int32)
        sources.append(source)
    for s in range(slots):
        tab_ref[s] = table_ref[sources[s]]

    group = 3

    def form(stage, between):
        for j in range(3):
            @pl.when(gets(j))
            def _():
                halo_copy(stage, j).wait_recv()

        def compress(at, carry):
            pieces = []
            for step in range(group):
                start = pl.multiple_of((at * group + step) * CBLOCK, CBLOCK)
                pieces.append(
                    jnp.concatenate(
                        [
                            ext_ref[stage, 0, :, pl.ds(start, window)],
                            ext_ref[stage, 1, :, pl.ds(start, window)],
                        ],
                        axis=1,
                    )
                )
            found = lax.dot_general(
                jnp.concatenate(pieces, axis=0), toep_ref[...], (((1,), (1,)), ((), ())),
                preferred_element_type=f32,
            ).astype(bf16)
            for step in range(group):
                start = pl.multiple_of((at * group + step) * CBLOCK, CBLOCK)
                one = found[step * rows : (step + 1) * rows]
                stacked = jnp.concatenate([one[:, :CBLOCK], one[:, CBLOCK:]], axis=0)
                sub = jnp.dot(steer, stacked, preferred_element_type=f32)
                sub_ref[:, pl.ds(start, CBLOCK)] = sub.astype(bf16).astype(f32)
            return carry

        lax.fori_loop(0, width // (CBLOCK * group), compress, 0)

        @pl.when(t == 0)
        def _():
            sub_ref[:, 0:EDGE] = jnp.zeros((256, EDGE), f32)

        between()

        def merge(a, carry):
            totals = [None, None]
            for c in range(2):
                x = sub_ref[pl.ds(pl.multiple_of((c * 16 + a) * 8, 8), 8), :]
                x_up = pltpu.roll(x, width - 1, 1)
                for parity in range(2):
                    b = 2 * a + parity
                    weight = coef_ref[0, c * 32 + b]
                    cosine = coef_ref[1, c * 32 + b]
                    sine = coef_ref[2, c * 32 + b]
                    y = (1.0 - weight) * x + weight * x_up
                    v = cosine * y + sine * pltpu.roll(y, 4, 0)
                    by = shift_ref[c, b]
                    z = pltpu.roll(v, jnp.where(by > 0, width - by, -by), 1)
                    z = z[:, EDGE : EDGE + range_dev]
                    totals[parity] = z if totals[parity] is None else totals[parity] + z
            both = jnp.where(
                iota((8, range_dev), 0) < 4, totals[0], pltpu.roll(totals[1], 4, 0)
            )
            merged_ref[pl.ds(pl.multiple_of(a * 8, 8), 8), :] = both
            return carry

        lax.fori_loop(0, 16, merge, 0)
        for f in range(blocks):
            part = jnp.dot(
                reorder, merged_ref[:, f * RBLOCK : (f + 1) * RBLOCK].astype(bf16),
                preferred_element_type=f32,
            )
            block_ref[f] = part.astype(bf16).reshape(4, 32, RBLOCK)
        for s in range(slots):
            kid_ref[stage * 4 : stage * 4 + 4, s] = block_ref[sources[s]]

    def spread_copy(k, d, peer, place):
        if k == CHUNKS:
            src = tab_ref.at[pl.ds(peer * CAP, CAP)]
            dst = tabs.at[pl.ds(place * CAP, CAP)]
        else:
            src = kid_ref.at[pl.ds(k * per, per), pl.ds(peer * CAP, CAP)]
            dst = kids.at[g, pl.ds(k * per, per), pl.ds(place * CAP, CAP)]
        return pltpu.make_async_remote_copy(
            src_ref=src, dst_ref=dst,
            send_sem=a2a_send.at[k, d - 1], recv_sem=a2a_recv.at[k, d - 1],
            device_id={"tile": peer}, device_id_type=MESH,
        )

    order = [CHUNKS] + list(range(CHUNKS))

    def spread_start(k):
        for d in range(1, tiles):
            spread_copy(k, d, lax.rem(t + d, tiles), t).start()

    def spread_wait(k):
        for d in range(1, tiles):
            peer = lax.rem(t + tiles - d, tiles)
            spread_copy(k, d, peer, peer).wait_recv()

    def line_copy(k, group, lane, to):
        if k == CHUNKS:
            part = packed_ref.at[group]
        else:
            part = kids.at[group, pl.ds(k * per, per)]
        return pltpu.make_async_remote_copy(
            src_ref=part, dst_ref=part,
            send_sem=line_send.at[lane, k], recv_sem=line_recv.at[group, k],
            device_id={"pulse": to}, device_id_type=MESH,
        )

    middle = spans // 2 * RBLOCK

    def part_copy(k, half, to):
        return pltpu.make_async_remote_copy(
            src_ref=part_ref.at[pl.ds(k * per, per), :, pl.ds(half * middle, middle)],
            dst_ref=arrived_ref.at[pl.ds(k * per, per), :, pl.ds(half * middle, middle)],
            send_sem=part_send.at[k, half], recv_sem=part_recv.at[k, half],
            device_id={"pulse": to}, device_id_type=MESH,
        )

    def prepare(group, beam_group, row, column, used):
        expand = (
            (iota((RBLOCK, lanes), 1) & (beams - 1)) + beam_group * beams
            == iota((RBLOCK, lanes), 0)
        ).astype(bf16)
        where_at = (iota((1, lanes), 1) // beams + 1).astype(f32)
        child = iota((32, lanes), 0).astype(f32)

        wide = jnp.dot(packed_ref[group], expand, preferred_element_type=f32)
        for at in range(slots // 4):
            pieces = []
            for slot in range(at * 4, at * 4 + 4):
                landing = wide[2 * slots + slot : 2 * slots + slot + 1, :]
                index = jnp.where(
                    (landing == where_at) & used, wide[slot : slot + 1, :], -9.0
                )
                frac = wide[slots + slot : slots + slot + 1, :]
                lower = (1.0 - frac).astype(bf16).astype(f32)
                weight = jnp.where(child == index, lower, 0.0)
                pieces.append(jnp.where(child == index + 1.0, frac, weight))
            block = jnp.concatenate(pieces, axis=0)
            at_column = pl.multiple_of(column + at * 128, 128)
            left_ref[row : row + lanes, pl.ds(at_column, 128)] = block.T.astype(bf16)

    def keep(k):
        if k == CHUNKS:
            tabs[pl.ds(t * CAP, CAP)] = tab_ref[pl.ds(t * CAP, CAP)]
        else:
            span = slice(k * per, (k + 1) * per)
            kids[g, span, pl.ds(t * CAP, CAP)] = kid_ref[span, pl.ds(t * CAP, CAP)]

    def begin_own(k):
        spread_wait(k)
        if k == CHUNKS:
            row, column = iota((3 * slots, slots * TABROWS), 0), iota((3 * slots, slots * TABROWS), 1)
            choose = column == (row & (slots - 1)) * TABROWS + row // slots
            packed_ref[g] = jnp.dot(
                choose.astype(bf16), tabs[...].reshape(slots * TABROWS, RBLOCK),
                preferred_element_type=f32,
            ).astype(bf16)
        line_copy(k, g, 0, inner).start()

    spread_start(CHUNKS)
    keep(CHUNKS)
    form(0, lambda: begin_own(CHUNKS))
    for k in range(CHUNKS // 2):
        spread_start(k)
        keep(k)

    def between():
        for k in range(CHUNKS // 2):
            begin_own(k)

    form(1, between)
    for k in range(CHUNKS // 2, CHUNKS):
        spread_start(k)
        keep(k)

    @pl.when(is_mid)
    def _():
        def relay(k):
            line_copy(k, end, 0, inner).wait_recv()
            line_copy(k, end, 1, inner).start()

        def finish(k):
            line_copy(k, inner, 0, inner).wait_recv()
            line_copy(k, far, 0, inner).wait_recv()

        relay(CHUNKS)
        relay(0)
        finish(CHUNKS)

        def prepare_group(group, carry):
            column = pl.multiple_of(group * depth, 128)
            prepare(group, g, 0, column, group >= 0)
            prepare(group, end, lanes, column, group != end)
            return carry

        lax.fori_loop(0, 4, prepare_group, 0)
        for k in range(1, CHUNKS // 2):
            relay(k)
        for k in range(CHUNKS // 2, CHUNKS):
            begin_own(k)
        for k in range(CHUNKS):
            if CHUNKS // 2 <= k + 1 < CHUNKS:
                relay(k + 1)
            finish(k)
            right = jnp.concatenate(
                [kids[:, k * per + i].reshape(4 * depth, RBLOCK) for i in range(per)], axis=1
            )
            for half in range(2):
                first = lanes + half * (lanes // 2)
                result = jnp.dot(
                    left_ref[first : first + lanes // 2, :], right, preferred_element_type=f32
                ).astype(bf16)
                for step in range(spans // 2):
                    w = half * (spans // 2) + step
                    for i in range(per):
                        part_ref[k * per + i, :, w * RBLOCK : (w + 1) * RBLOCK] = result[
                            step * beams : (step + 1) * beams, i * RBLOCK : (i + 1) * RBLOCK
                        ]
                part_copy(k, half, end).start()
            result = jnp.dot(
                left_ref[:lanes, :], right, preferred_element_type=f32
            ).astype(bf16)
            for w in range(spans):
                for i in range(per):
                    out_ref[out_at(k * per + i), :, w * RBLOCK : (w + 1) * RBLOCK] = result[
                        w * beams : (w + 1) * beams, i * RBLOCK : (i + 1) * RBLOCK
                    ]
        for k in order:
            line_copy(k, g, 0, inner).wait_send()
            line_copy(k, end, 1, inner).wait_send()
        for k in range(CHUNKS):
            for half in range(2):
                part_copy(k, half, end).wait_send()

    @pl.when(jnp.logical_not(is_mid))
    def _():
        for k in range(CHUNKS // 2, CHUNKS):
            begin_own(k)
        prepare(g, g, 0, 0, g >= 0)
        for k in range(CHUNKS):
            right = jnp.concatenate(
                [kids[g, k * per + i].reshape(depth, RBLOCK) for i in range(per)], axis=1
            )
            result = jnp.dot(
                left_ref[:lanes, :depth], right, preferred_element_type=f32
            )
            for w in range(spans):
                for i in range(per):
                    own_ref[k * per + i, :, w * RBLOCK : (w + 1) * RBLOCK] = result[
                        w * beams : (w + 1) * beams, i * RBLOCK : (i + 1) * RBLOCK
                    ]
        for k in range(CHUNKS):
            for half in range(2):
                part_copy(k, half, inner).wait_recv()
                span = slice(half * middle, (half + 1) * middle)
                for i in range(per):
                    x = k * per + i
                    out_ref[out_at(x), :, span] = (
                        own_ref[x, :, span] + arrived_ref[x, :, span].astype(f32)
                    ).astype(bf16)
        for k in order:
            line_copy(k, g, 0, inner).wait_send()

    for k in order:
        for d in range(1, tiles):
            spread_copy(k, d, lax.rem(t + d, tiles), t).wait_send()
    for stage in range(STAGES):
        for j in range(3):
            @pl.when(sends(j))
            def _():
                halo_copy(stage, j).wait_send()


def fused(shift, coef, foot, echoes, replica, steer, tables, tiles, beams, range_dev):
    slots = tiles * CAP
    lanes = range_dev // RBLOCK * beams
    bf16 = jnp.bfloat16
    vmem = pl.BlockSpec(memory_space=pltpu.VMEM)
    smem = pl.BlockSpec(memory_space=pltpu.SMEM)
    dma = pltpu.SemaphoreType.DMA
    return pl.pallas_call(
        functools.partial(fused_kernel, tiles),
        out_shape=jax.ShapeDtypeStruct((8, beams, range_dev), bf16),
        in_specs=[smem] * 3 + [vmem] * 4,
        out_specs=vmem,
        scratch_shapes=[
            pltpu.VMEM((STAGES, 2, echoes.shape[2], 2 * range_dev + 2 * EDGE), bf16),
            pltpu.VMEM((2 * CBLOCK, 2 * (CBLOCK + replica.shape[1])), bf16),
            pltpu.VMEM((256, range_dev + CBLOCK), jnp.float32),
            pltpu.VMEM((128, range_dev), jnp.float32),
            pltpu.VMEM((slots, 4, 32, RBLOCK), bf16),
            pltpu.VMEM((8, slots, 32, RBLOCK), bf16),
            pltpu.VMEM((slots, TABROWS, RBLOCK), bf16),
            pltpu.VMEM((4, 8, slots, 32, RBLOCK), bf16),
            pltpu.VMEM((slots, TABROWS, RBLOCK), bf16),
            pltpu.VMEM((4, 3 * slots, RBLOCK), bf16),
            pltpu.VMEM((2 * lanes, 4 * slots * 32), bf16),
            pltpu.VMEM((8, beams, range_dev), bf16),
            pltpu.VMEM((8, beams, range_dev), bf16),
            pltpu.VMEM((8, beams, range_dev), jnp.float32),
            dma((STAGES, 3)),
            dma((STAGES, 3)),
            dma((CHUNKS + 1, tiles - 1)),
            dma((CHUNKS + 1, tiles - 1)),
            dma((2, CHUNKS + 1)),
            dma((4, CHUNKS + 1)),
            dma((CHUNKS, 2)),
            dma((CHUNKS, 2)),
        ],
        compiler_params=pltpu.CompilerParams(
            collective_id=0, has_side_effects=True, vmem_limit_bytes=56 << 20
        ),
    )(shift, coef, foot, echoes, replica, steer, tables)


def shards(
    echoes, replica, steer_phase, range_shift, merge_phase, merge_frac,
    footprint, row_slot, beam_index, beam_frac,
):
    pulse_count, pol_count, range_dev = echoes.shape[1:]
    rows = pulse_count * pol_count
    taps = replica.shape[1]
    final_beams = beam_index.shape[2]
    tiles = lax.axis_size("tile")
    groups = lax.axis_size("pulse")
    slot_count = tiles * CAP
    scale = 1.0 / math.sqrt(steer_phase.shape[1])
    steer_re = jnp.cos(steer_phase) * scale
    steer_im = jnp.sin(steer_phase) * scale
    steer = jnp.concatenate(
        [
            jnp.concatenate([steer_re, -steer_im], axis=1),
            jnp.concatenate([steer_im, steer_re], axis=1),
        ],
        axis=0,
    ).astype(jnp.bfloat16)
    half_root = math.sqrt(0.5)
    coef = jnp.stack(
        [
            merge_frac.reshape(-1),
            (jnp.cos(merge_phase) * half_root).reshape(-1),
            (jnp.sin(merge_phase) * half_root).reshape(-1),
        ]
    )
    beams = final_beams // groups
    if groups == 4 and slot_count == range_dev // RBLOCK:
        split = echoes.transpose(0, 2, 1, 3).reshape(2, STAGES, rows // STAGES, range_dev)
        landing = jnp.broadcast_to(row_slot[0][:, None] + 1, beam_index.shape[1:])
        tables = jnp.stack(
            [beam_index[0].astype(jnp.float32), beam_frac[0].astype(jnp.float32),
             landing.astype(jnp.float32)], axis=1,
        )
        tables = jnp.pad(tables, ((0, 0), (0, TABROWS - 3), (0, 0))).astype(jnp.bfloat16)
        image = fused(
            range_shift, coef, footprint, split, replica, steer, tables,
            tiles, beams, range_dev,
        )
        return image.reshape(2, pol_count, beams, range_dev)
    own = echoes.reshape(2, rows, range_dev)
    following = shifted(own, "tile", -1)
    before = shifted(own[:, :, range_dev - EDGE :], "tile", 1)
    after = shifted(own[:, :, :EDGE], "tile", -2)

    width = range_dev + CBLOCK
    smem = pl.BlockSpec(memory_space=pltpu.SMEM)
    vmem = pl.BlockSpec(memory_space=pltpu.VMEM)
    kids, tabs = pl.pallas_call(
        form_kernel,
        out_shape=(
            jax.ShapeDtypeStruct((8, slot_count, 32, RBLOCK), jnp.bfloat16),
            jax.ShapeDtypeStruct((slot_count, TABROWS, RBLOCK), jnp.bfloat16),
        ),
        in_specs=[smem] * 4 + [vmem] * 8,
        out_specs=(vmem, vmem),
        scratch_shapes=[
            pltpu.VMEM((2, rows, 2 * range_dev + 2 * EDGE), jnp.bfloat16),
            pltpu.VMEM((2 * CBLOCK, 2 * (CBLOCK + taps)), jnp.bfloat16),
            pltpu.VMEM((256, width), jnp.float32),
            pltpu.VMEM((256, range_dev), jnp.bfloat16),
        ],
        compiler_params=pltpu.CompilerParams(vmem_limit_bytes=56 << 20),
    )(
        range_shift, coef, footprint, row_slot,
        own, following, before, after, replica, steer, beam_index, beam_frac,
    )
    sent = jnp.concatenate(
        [kids.transpose(1, 0, 2, 3).reshape(slot_count, 256, RBLOCK), tabs], axis=1
    )
    got = lax.all_to_all(
        sent.reshape(tiles, CAP, 256 + TABROWS, RBLOCK), "tile",
        split_axis=0, concat_axis=0, tiled=True,
    ).reshape(slot_count, 256 + TABROWS, RBLOCK)
    gathered = lax.all_gather(got, "pulse", axis=0, tiled=True)
    total_slots = groups * slot_count
    image = pl.pallas_call(
        place_kernel,
        out_shape=jax.ShapeDtypeStruct((2 * pol_count, beams, range_dev), jnp.bfloat16),
        in_specs=[vmem],
        out_specs=vmem,
        scratch_shapes=[
            pltpu.VMEM((total_slots * 32, range_dev // RBLOCK * beams), jnp.bfloat16),
            pltpu.VMEM((total_slots * 32, 8 * RBLOCK), jnp.bfloat16),
        ],
        compiler_params=pltpu.CompilerParams(vmem_limit_bytes=56 << 20),
    )(gathered)
    return image.reshape(2, pol_count, beams, range_dev)


def solution(mesh):
    placed = (
        P(None, "pulse", None, "tile"),
        P(),
        P(),
        P(),
        P(),
        P(),
        P("pulse", "tile"),
        P("pulse", "tile"),
        P("pulse", "tile", None),
        P("pulse", "tile", None),
    )
    return jax.shard_map(
        shards,
        mesh=mesh,
        in_specs=placed,
        out_specs=P(None, None, "pulse", "tile"),
        check_vma=False,
    )
```
